512 devices in a mesh: lon: 16 (over x, z_lo), lat: 4 (over z_hi, core), age: 8 (over y).
Axes of the slice: x: 4, y: 8, z: 8 (z_hi: 2, z_lo: 4; z = z_hi * 4 + z_lo), core: 2. Of those that a mesh axis runs over, the one named last changes fastest.
Arguments:
- density: float32 [64, 256, 4096], P('age', 'lat', 'lon'), may hold values from 0.1 to 3
- adjoint_next: float32 [64, 256, 4096], P('age', 'lat', 'lon'), may hold values from -6 to 6
- current_east: float32 [256, 4096], P('lat', 'lon'), may hold values from -0.25 to 0.25
- current_north: float32 [256, 4096], P('lat', 'lon'), may hold values from -0.25 to 0.25
- swim_speed: float32 [64], P('age'), may hold values from 0.3 to 1
- diffusion: float32 [64], P('age'), may hold values from 0.05 to 0.12
- mortality: float32 [64], P('age'), may hold values from 0.1 to 0.6
- cohort_mass: float32 [64], P('age'), may hold values from 0.2 to 2
- selectivity: float32 [8, 64], P(None, 'age'), may hold values from 0 to 1
- effort: float32 [8, 256, 4096], P(None, 'lat', 'lon'), may hold values from 0.01 to 0.5
- catch_mask: int32 [8, 256, 4096], P(None, 'lat', 'lon'), may hold values 0 or 1
- region: int32 [256, 4096], P('lat', 'lon'), may hold values from 0 to 15
- sea_mask: int32 [256, 4096], P('lat', 'lon'), may hold values 0 or 1
- habitat: float32 [256, 4096], P('lat', 'lon'), may hold values from 0.5 to 1
- observed: float32 [8, 16], replicated, may hold values from 0.3 to 3
Outputs:
- grad_density: float32 [64, 256, 4096], P('age', 'lat', 'lon')
The draws below stay inside these ranges and needn't reach their ends.
All inputs are finite; a program needn't handle non-finite values. No bound on the sum of `catch_mask` or of `sea_mask` on one device may be relied on, other than what follows from the above.
Results may differ from the reference program's by a relative error of at most 0.000096.
Values sent between devices are 32-bit elements; how exact they have to be, the bound alone decides.
No kernel may reach another device: no remote copies, remote signals or barrier semaphores. Data moves between devices by JAX's collectives and lax.ppermute only.
A program may use at most 64 MiB of HBM per device.

```python
import math
import jax
import jax.numpy as jnp
from jax import lax

FLEETS = 8
REGIONS = 16
COHORTS = 64
NLAT = 256
NLON = 4096


def place_ends(drawn, key, low, top_value):
    extent = drawn.shape
    index_at = [jax.random.randint(jax.random.fold_in(key, axis), (), 0, extent[axis]) for axis in range(len(extent))]
    drawn = drawn.at[tuple(index_at)].set(low)
    longest = extent.index(max(extent))
    index_at[longest] = (index_at[longest] + 1) % extent[longest]
    return drawn.at[tuple(index_at)].set(top_value)


def block_scale(rng, shape, pieces, smallest, top_value):
    loudness, own = 1.0, jax.random.fold_in(rng, 6)
    for dim, parts in pieces:
        heights = jnp.exp(jax.random.uniform(jax.random.fold_in(own, dim), (parts,), jnp.float32, smallest / len(pieces), top_value / len(pieces)))
        loudness = loudness * jnp.repeat(heights, shape[dim] // parts).reshape([-1 if axis == dim else 1 for axis in range(len(shape))])
    return loudness


def gaussian(key, extent, width, most, cuts=(), kind=jnp.bfloat16):
    result = jax.random.normal(key, extent, jnp.float32) * width
    if len(cuts) > 0:
        result = block_scale(key, extent, cuts, -0.22, 0.18) * result
    return jnp.clip(result, min=-most, max=most).astype(kind)


def setup_inputs(seed: int = 0) -> dict:
    keys = jax.random.split(jax.random.key(seed), 16)
    return {
        "density": jnp.clip(jnp.exp(math.log(3.0) - 3.4011974 * jax.random.uniform(keys[0], (COHORTS, NLAT, NLON), jnp.float32) ** block_scale(keys[0], (COHORTS, NLAT, NLON), ((0, 8), (1, 4), (2, 16)), -0.2, 0.2)), 0.1, 3.0),
        "adjoint_next": gaussian(keys[1], (COHORTS, NLAT, NLON), 1.0, 6.0, ((0, 8), (1, 4), (2, 16)), jnp.float32),
        "current_east": jnp.clip(jax.random.uniform(keys[2], (NLAT, NLON), jnp.float32, -0.25, 0.25) * block_scale(keys[2], (NLAT, NLON), ((0, 4), (1, 16)), -0.4, 0.0), -0.25, 0.25),
        "current_north": jnp.clip(jax.random.uniform(keys[3], (NLAT, NLON), jnp.float32, -0.25, 0.25) * block_scale(keys[3], (NLAT, NLON), ((0, 4), (1, 16)), -0.4, 0.0), -0.25, 0.25),
        "swim_speed": jnp.clip(jnp.exp(math.log(1.0) - 1.2039728 * jax.random.uniform(keys[4], (COHORTS,), jnp.float32) ** block_scale(keys[4], (COHORTS,), ((0, 8),), -0.2, 0.2)), 0.3, 1.0),
        "diffusion": jnp.clip(0.05 + 0.06999999657273293 * jax.random.uniform(keys[5], (COHORTS,), jnp.float32) ** block_scale(keys[5], (COHORTS,), ((0, 8),), -0.2, 0.2), 0.05, 0.12),
        "mortality": jnp.clip(jnp.exp(math.log(0.6) - 1.7917595 * jax.random.uniform(keys[6], (COHORTS,), jnp.float32) ** block_scale(keys[6], (COHORTS,), ((0, 8),), -0.2, 0.2)), 0.1, 0.6),
        "cohort_mass": jnp.clip(jnp.exp(math.log(2.0) - 2.3025851 * jax.random.uniform(keys[7], (COHORTS,), jnp.float32) ** block_scale(keys[7], (COHORTS,), ((0, 8),), -0.2, 0.2)), 0.2, 2.0),
        "selectivity": jnp.clip(1.0 * jax.random.uniform(keys[8], (FLEETS, COHORTS), jnp.float32) ** block_scale(keys[8], (FLEETS, COHORTS), ((1, 8),), -0.2, 0.2), 0.0, 1.0),
        "effort": jnp.clip(jnp.exp(math.log(0.5) - 3.912023 * jax.random.uniform(keys[9], (FLEETS, NLAT, NLON), jnp.float32) ** block_scale(keys[9], (FLEETS, NLAT, NLON), ((1, 4), (2, 16)), -0.2, 0.2)), 0.01, 0.5),
        "catch_mask": place_ends((jax.random.randint(keys[10], (FLEETS, NLAT, NLON), 0, 2) < 1).astype(jnp.int32), jax.random.fold_in(keys[10], 1), 0, 1),
        "region": place_ends(jax.random.randint(keys[11], (NLAT, NLON), 0, REGIONS), jax.random.fold_in(keys[11], 1), 0, REGIONS - 1).astype(jnp.int32),
        "sea_mask": place_ends((jax.random.randint(keys[12], (NLAT, NLON), 0, 5) < 4).astype(jnp.int32), jax.random.fold_in(keys[12], 1), 0, 1),
        "habitat": jnp.clip(0.5 + 0.5 * jax.random.uniform(keys[13], (NLAT, NLON), jnp.float32) ** block_scale(keys[13], (NLAT, NLON), ((0, 4), (1, 16)), -0.2, 0.2), 0.5, 1.0),
        "observed": jnp.clip(jnp.exp(jax.random.uniform(keys[14], (FLEETS, REGIONS), jnp.float32, math.log(0.3), math.log(3.0))), 0.3, 3.0),
    }


def coeffs(current_east, current_north, swim_speed, diffusion):
    flow_east = swim_speed[:, None, None] * current_east[None]
    flow_north = swim_speed[:, None, None] * current_north[None]
    spread = diffusion[:, None, None]
    to_east = spread + jnp.maximum(-flow_east, 0.0)
    to_west = spread + jnp.maximum(flow_east, 0.0)
    to_north = spread + jnp.maximum(-flow_north, 0.0)
    to_south = spread + jnp.maximum(flow_north, 0.0)
    centre = 1.0 - (to_east + to_west + to_north + to_south)
    return (centre, to_east, to_west, to_north, to_south)

def transport(field, coefs, sea):
    centre, to_east, to_west, to_north, to_south = coefs
    zero_row = jnp.zeros_like(field[:, :1])
    from_east = jnp.roll(field, -1, axis=2)
    from_west = jnp.roll(field, 1, axis=2)
    from_north = jnp.concatenate([field[:, 1:], zero_row], axis=1)
    from_south = jnp.concatenate([zero_row, field[:, :-1]], axis=1)
    return sea * (centre * field + to_east * from_east + to_west * from_west + to_north * from_north + to_south * from_south)

def reference(density, adjoint_next, current_east, current_north, swim_speed, diffusion, mortality, cohort_mass, selectivity, effort, catch_mask, region, sea_mask, habitat, observed):
    sea = sea_mask.astype(jnp.float32)[None]
    coefs = coeffs(current_east, current_north, swim_speed, diffusion)
    onehot = (region[None] == jnp.arange(REGIONS, dtype=jnp.int32)[:, None, None]).astype(jnp.float32)
    reported = catch_mask.astype(jnp.float32)
    unit = REGIONS / (NLAT * NLON)
    highest = lax.Precision.HIGHEST

    def objective(start):
        midway = transport(start, coefs, sea)
        settled = transport(midway, coefs, sea)
        weighted = cohort_mass[:, None, None] * settled
        running = jnp.cumsum(weighted, axis=0)
        older = running[-1][None] - running
        fishing = jnp.einsum('fa,fxy->axy', selectivity, effort, precision=highest)
        total_mort = mortality[:, None, None] + fishing + 0.02 * older
        survive = jnp.exp(-total_mort)
        yield_frac = (1.0 - survive) / total_mort
        landed = cohort_mass[:, None, None] * yield_frac * settled
        by_fleet = jnp.einsum('fa,axy->fxy', selectivity, landed, precision=highest) * effort * reported
        predicted = unit * jnp.einsum('fxy,rxy->fr', by_fleet, onehot, precision=highest)
        loss = jnp.sum(predicted - observed * jnp.log(1.0 + predicted)) / unit
        kept = habitat[None] * survive * settled
        aged = jnp.concatenate([kept[:-2], (kept[-2] + kept[-1])[None]], axis=0)
        return loss + jnp.sum(adjoint_next[1:] * aged)
    return jax.grad(objective)(density)
```

```python
import functools

import jax
import jax.numpy as jnp
from jax import lax
from jax.experimental import pallas as pl
from jax.experimental.pallas import tpu as pltpu
from jax.sharding import PartitionSpec as P

ROWS, COLS = 64, 256
EROWS, ECOLS = ROWS + 8, COLS + 128
LANES = 128
N = 8
WIDE, NARROW = 4, 2
DENSITY, EAST, NORTH, SEA = 0, 32, 36, 40
ADJOINT, EFFORT, MASK, REGION, HABITAT = 44, 60, 76, 92, 94
STRIP = 96
PACKED = 2 * EROWS + 8
F32 = jnp.float32


def every_field(density, adjoint, effort, mask, east, north, region, sea, habitat):
    for c in range(N):
        yield density, c, DENSITY + WIDE * c, WIDE
    yield east, None, EAST, WIDE
    yield north, None, NORTH, WIDE
    yield sea, None, SEA, WIDE
    for c in range(N):
        yield adjoint, c, ADJOINT + NARROW * c, NARROW
    for f in range(N):
        yield effort, f, EFFORT + NARROW * f, NARROW
    for f in range(N):
        yield mask, f, MASK + NARROW * f, NARROW
    yield region, None, REGION, NARROW
    yield habitat, None, HABITAT, NARROW


def part(ref, index, rows, cols):
    block = ref[rows, cols] if index is None else ref[index, rows, cols]
    return block.astype(F32)


def lane_iota(rows):
    return lax.broadcasted_iota(jnp.int32, (rows, LANES), 1)


def turned(block, by):
    by = by % LANES
    return block if by == 0 else pltpu.roll(block, by, 1)


def pack_kernel(*refs):
    inputs, (to_east, to_west, to_north, to_south) = refs[:9], refs[9:]
    lane = lane_iota(ROWS)
    everything = slice(0, ROWS)
    right = jnp.zeros((ROWS, LANES), F32)
    left = jnp.zeros((ROWS, LANES), F32)
    for ref, index, place, width in every_field(*inputs):
        here = (lane >= place) & (lane < place + width)
        right = jnp.where(here, turned(part(ref, index, everything, slice(LANES, COLS)), place + width), right)
        left = jnp.where(here, turned(part(ref, index, everything, slice(0, LANES)), place), left)
        columns = slice(0, COLS)
        to_north[place : place + width, :] = part(ref, index, slice(ROWS - width, ROWS), columns)
        to_south[place : place + width, :] = part(ref, index, slice(0, width), columns)
    to_east[...] = right
    to_west[...] = left


def corner_kernel(north_in, south_in, west_low, west_high, east_low, east_high, to_north, to_south):
    del north_in, south_in
    to_north[...] = jnp.zeros((8, COLS), F32)
    to_south[...] = jnp.zeros((8, COLS), F32)
    to_north[0:4, 0:LANES] = west_high[4:8, :]
    to_north[0:4, LANES:COLS] = east_high[4:8, :]
    to_south[0:4, 0:LANES] = west_low[0:4, :]
    to_south[0:4, LANES:COLS] = east_low[0:4, :]


def spill(total, out, count):
    side_lane = lane_iota(8)
    packed = jnp.zeros((8, LANES), F32)
    for k in range(EROWS // 8):
        side = total[8 * k : 8 * k + 8, COLS:ECOLS]
        here = (side_lane >= 4 * k) & (side_lane < 4 * k + 4)
        packed = jnp.where(here, turned(side, 4 * k + 2), packed)
    first, second = total[:, 0:LANES], total[:, LANES:COLS]

    for slot in range(count):
        out[slot, 0:EROWS, :] = first
        out[slot, EROWS : 2 * EROWS, :] = second
        out[slot, 2 * EROWS : PACKED, :] = packed


def gathered(received, keep, out):
    total = jnp.zeros((PACKED, LANES), F32)
    for slot in range(received.shape[0]):
        total = total + jnp.where(keep(slot), received[slot], 0.0)
    out[:, 0:LANES] = total[0:EROWS]
    out[:, LANES:COLS] = total[EROWS : 2 * EROWS]
    packed = total[2 * EROWS : PACKED]
    side_lane = lane_iota(8)
    here = (side_lane < NARROW) | (side_lane >= LANES - NARROW)
    for k in range(EROWS // 8):
        out[8 * k : 8 * k + 8, COLS:ECOLS] = jnp.where(here, turned(packed, -(4 * k + 2)), 0.0)


def coeffs(east, north, swim, spread):
    flow_east = swim * east
    flow_north = swim * north
    to_east = spread + jnp.maximum(-flow_east, 0.0)
    to_west = spread + jnp.maximum(flow_east, 0.0)
    to_north = spread + jnp.maximum(-flow_north, 0.0)
    to_south = spread + jnp.maximum(flow_north, 0.0)
    centre = 1.0 - (to_east + to_west + to_north + to_south)
    return centre, to_east, to_west, to_north, to_south


def ahead(x, axis):
    return pltpu.roll(x, x.shape[axis] - 1, axis)


def behind(x, axis):
    return pltpu.roll(x, 1, axis)


def advance(u, coefs, sea):
    centre, to_east, to_west, to_north, to_south = coefs
    return sea * (
        centre * u + to_east * ahead(u, 1) + to_west * behind(u, 1) + to_north * ahead(u, 0) + to_south * behind(u, 0)
    )


def retreat(v, coefs):
    centre, to_east, to_west, to_north, to_south = coefs
    return (
        centre * v + behind(to_east * v, 1) + ahead(to_west * v, 1) + behind(to_north * v, 0) + ahead(to_south * v, 0)
    )


def settle_kernel(*refs):
    inputs = refs[:9]
    west_in, east_in, north_in, south_in, swim, spread, mass = refs[9:16]
    settled_out, total_out, tail_out, adjoint_out, effort_out, mask_out, fields_out = refs[16:23]
    density_ext, west, east, total = refs[23:]
    outs = {}
    for c in range(N):
        outs[DENSITY + WIDE * c] = density_ext.at[c]
        outs[ADJOINT + NARROW * c] = adjoint_out.at[c]
        outs[EFFORT + NARROW * c] = effort_out.at[c]
        outs[MASK + NARROW * c] = mask_out.at[c]
    for k, place in enumerate((EAST, NORTH, SEA, REGION, HABITAT)):
        outs[place] = fields_out.at[k]
    west[0:ROWS, :] = west_in[...]
    east[0:ROWS, :] = east_in[...]
    west[ROWS : ROWS + 4, :] = north_in[STRIP : STRIP + 4, 0:LANES]
    east[ROWS : ROWS + 4, :] = north_in[STRIP : STRIP + 4, LANES:COLS]
    west[ROWS + 4 : EROWS, :] = south_in[STRIP : STRIP + 4, 0:LANES]
    east[ROWS + 4 : EROWS, :] = south_in[STRIP : STRIP + 4, LANES:COLS]
    lane = lane_iota(EROWS)
    for ref, index, place, width in every_field(*inputs):
        out = outs[place]
        out[0:ROWS, 0:COLS] = part(ref, index, slice(0, ROWS), slice(0, COLS))
        if width < 4:
            out[ROWS:EROWS, 0:COLS] = jnp.zeros((8, COLS), F32)
        out[ROWS : ROWS + width, 0:COLS] = north_in[place : place + width, :]
        out[EROWS - width : EROWS, 0:COLS] = south_in[place : place + width, :]
        side = jnp.where(lane < width, turned(east[...], -place), 0.0)
        side = jnp.where(lane >= LANES - width, turned(west[...], LANES - width - place), side)
        out[:, COLS:ECOLS] = side
    tail_out[...] = adjoint_out[0]
    total[...] = jnp.zeros((EROWS, ECOLS), F32)

    def cohort(c, carry):
        sea = fields_out[2]
        coefs = coeffs(fields_out[0], fields_out[1], swim[c], spread[c])
        settled = advance(advance(density_ext[c], coefs, sea), coefs, sea)
        settled_out[c] = settled
        total[...] += mass[c] * settled
        return carry

    lax.fori_loop(0, N, cohort, 0)
    spill(total[...], total_out, total_out.shape[0])


def catch_kernel(
    age, received, settled, tail, adjoint, effort, mask, fields, mortality, mass, selectivity,
    kept_out, yield_out, slope_out, catch_out, older, fleets,
):
    shard = age[0]
    last = shard == age[1] - 1
    gathered(received, lambda slot: slot > shard, older)

    def strip(t, carry):
        rows = pl.ds(pl.multiple_of(t * 8, 8), 8)
        harvest = [effort[f, rows, :] for f in range(N)]
        habitat = fields[4, rows, :]
        run = older[rows, :]
        taken = [jnp.zeros((8, COLS), F32) for _ in range(N)]
        for c in reversed(range(N)):
            settled_c = settled[c, rows, :]
            total_mort = mortality[c] + 0.02 * run
            for f in range(N):
                total_mort = total_mort + selectivity[f, c] * harvest[f]
            survive = jnp.exp(-total_mort)
            inverse = 1.0 / total_mort
            yield_frac = (1.0 - survive) * inverse
            if c + 1 < N:
                carried = adjoint[c + 1, rows, :]
            else:
                carried = jnp.where(last, adjoint[c, rows, :], tail[rows, :])
            weighted = mass[c] * settled_c
            kept_out[c, rows, :] = carried * habitat * survive
            yield_out[c, rows, :] = mass[c] * yield_frac
            slope_out[c, rows, :] = weighted * (survive - yield_frac) * inverse
            landed = (weighted * yield_frac)[:, 0:COLS]
            for f in range(N):
                taken[f] = taken[f] + selectivity[f, c] * landed
            run = run + weighted
        for f in range(N):
            fleets[f, rows, :] = taken[f] * (harvest[f] * mask[f, rows, :])[:, 0:COLS]
        return carry

    lax.fori_loop(0, EROWS // 8, strip, 0)
    lane = lane_iota(N)
    fleet = lax.broadcasted_iota(jnp.int32, (N, LANES), 0)

    def one_region(r, table):
        sums = [jnp.zeros((8, LANES), F32) for _ in range(N)]
        for t in range(ROWS // 8):
            for half in range(2):
                rows, cols = slice(8 * t, 8 * t + 8), slice(LANES * half, LANES * half + LANES)
                here = fields[3, rows, cols] == r.astype(F32)
                for f in range(N):
                    sums[f] = sums[f] + jnp.where(here, fleets[f, rows, cols], 0.0)
        for f in range(N):
            column = jnp.sum(sums[f], axis=0, keepdims=True)
            column = jnp.sum(column, axis=1, keepdims=True)
            table = jnp.where((fleet == f) & (lane == r + 16 * f), column, table)
        return table

    table = lax.fori_loop(0, 16, one_region, jnp.zeros((N, LANES), F32))
    row = jnp.sum(table, axis=0, keepdims=True)
    catch_out[...] = jnp.broadcast_to(row, catch_out.shape)


def press_kernel(
    catches, observed, settled, effort, mask, fields, kept, yields, slope, selectivity,
    base_out, press_out, total_out, total, *, unit,
):
    predicted = jnp.sum(catches[...], axis=0, keepdims=True) * unit
    misfit = jnp.broadcast_to(1.0 - observed[...] / (1.0 + predicted), (8, LANES))

    def strip(t, carry):
        rows = pl.ds(pl.multiple_of(t * 8, 8), 8)
        region = fields[3, rows, :].astype(jnp.int32)
        spread_back = []
        for f in range(N):
            picked = [
                jnp.take_along_axis(misfit, region[:, LANES * k : LANES * k + LANES] + 16 * f, axis=1)
                for k in range(ECOLS // LANES)
            ]
            spread_back.append(jnp.concatenate(picked, axis=1) * effort[f, rows, :] * mask[f, rows, :])
        run = jnp.zeros((8, ECOLS), F32)
        for c in range(N):
            pull = selectivity[0, c] * spread_back[0]
            for f in range(1, N):
                pull = pull + selectivity[f, c] * spread_back[f]
            kept_c = kept[c, rows, :]
            pressure = slope[c, rows, :] * pull - kept_c * settled[c, rows, :]
            base_out[c, rows, :] = kept_c + yields[c, rows, :] * pull
            press_out[c, rows, :] = run
            run = run + pressure
        total[rows, :] = run
        return carry

    lax.fori_loop(0, EROWS // 8, strip, 0)
    spill(total[...], total_out, total_out.shape[0])


def retreat_kernel(age, received, base, press, fields, swim, spread, mass, grad_out, younger):
    shard = age[0]
    gathered(received, lambda slot: slot < shard, younger)

    def cohort(c, carry):
        sea = fields[2]
        coefs = coeffs(fields[0], fields[1], swim[c], spread[c])
        settled_bar = base[c] + (0.02 * mass[c]) * (younger[...] + press[c])
        middle_bar = retreat(sea * settled_bar, coefs)
        grad_out[c] = retreat(sea * middle_bar, coefs)[0:ROWS, 0:COLS]
        return carry

    lax.fori_loop(0, N, cohort, 0)


VMEM = pl.BlockSpec(memory_space=pltpu.VMEM)
SMEM = pl.BlockSpec(memory_space=pltpu.SMEM)


def shape(*dims):
    return jax.ShapeDtypeStruct(dims, F32)


def call(kernel, name, in_specs, outs, scratch=()):
    return pl.pallas_call(
        kernel,
        name=name,
        in_specs=in_specs,
        out_specs=[VMEM] * len(outs),
        out_shape=outs,
        scratch_shapes=[pltpu.VMEM(dims, F32) for dims in scratch],
    )


def local(
    density, adjoint_next, current_east, current_north, swim_speed, diffusion, mortality, cohort_mass,
    selectivity, effort, catch_mask, region, sea_mask, habitat, observed,
):
    lons, lats, ages = (lax.axis_size(axis) for axis in ("lon", "lat", "age"))
    devices = lons * lats * ages
    age = jnp.stack([lax.axis_index("age"), jnp.int32(ages)])
    inputs = (density, adjoint_next, effort, catch_mask, current_east, current_north, region, sea_mask, habitat)
    strip_rows = STRIP + 8

    to_east, to_west, to_north, to_south = call(
        pack_kernel,
        "pack",
        [VMEM] * 9,
        [shape(ROWS, LANES), shape(ROWS, LANES), shape(strip_rows, COLS), shape(strip_rows, COLS)],
    )(*inputs)
    from_west = lax.ppermute(to_east, "lon", [(i, (i + 1) % lons) for i in range(lons)])
    from_east = lax.ppermute(to_west, "lon", [((i + 1) % lons, i) for i in range(lons)])
    low = pl.BlockSpec((8, LANES), lambda i: (0, 0))
    high = pl.BlockSpec((8, LANES), lambda i: (ROWS // 8 - 1, 0))
    corner = pl.BlockSpec((8, COLS), lambda i: (STRIP // 8, 0))
    to_north, to_south = pl.pallas_call(
        corner_kernel,
        name="corner",
        grid=(1,),
        in_specs=[pl.BlockSpec(memory_space=pl.ANY)] * 2 + [low, high, low, high],
        out_specs=[corner, corner],
        out_shape=[shape(strip_rows, COLS)] * 2,
        input_output_aliases={0: 0, 1: 1},
    )(to_north, to_south, from_west, from_west, from_east, from_east)
    from_south = lax.ppermute(to_north, "lat", [(i, i + 1) for i in range(lats - 1)])
    from_north = lax.ppermute(to_south, "lat", [(i + 1, i) for i in range(lats - 1)])

    stack = shape(N, EROWS, ECOLS)
    summed = shape(ages, PACKED, LANES)
    extended = (EROWS, ECOLS)
    settled, totals, tail, adjoint_ext, effort_ext, mask_ext, fields = call(
        settle_kernel,
        "settle",
        [VMEM] * 13 + [SMEM] * 3,
        [stack, summed, shape(*extended), stack, stack, stack, shape(5, *extended)],
        [(N, *extended), (EROWS, LANES), (EROWS, LANES), extended],
    )(*inputs, from_west, from_east, from_north, from_south, swim_speed, diffusion, cohort_mass)
    tail = lax.ppermute(tail, "age", [(i + 1, i) for i in range(ages - 1)])
    totals = lax.all_to_all(totals, "age", 0, 0, tiled=True)

    kept, yields, slope, catches = call(
        catch_kernel,
        "catch",
        [SMEM] + [VMEM] * 7 + [SMEM] * 3,
        [stack, stack, stack, shape(devices, LANES)],
        [extended, (N, EROWS, COLS)],
    )(age, totals, settled, tail, adjoint_ext, effort_ext, mask_ext, fields, mortality, cohort_mass, selectivity)
    catches = lax.all_to_all(catches, ("lon", "lat", "age"), 0, 0, tiled=True)

    unit = observed.shape[1] / (ROWS * COLS * lons * lats)
    base, press, totals = call(
        functools.partial(press_kernel, unit=unit),
        "press",
        [VMEM] * 9 + [SMEM],
        [stack, stack, summed],
        [extended],
    )(catches, observed.reshape(1, LANES), settled, effort_ext, mask_ext, fields, kept, yields, slope, selectivity)
    totals = lax.all_to_all(totals, "age", 0, 0, tiled=True)

    (grad,) = call(
        retreat_kernel,
        "retreat",
        [SMEM] + [VMEM] * 4 + [SMEM] * 3,
        [shape(N, ROWS, COLS)],
        [extended],
    )(age, totals, base, press, fields, swim_speed, diffusion, cohort_mass)
    return grad


def solution(mesh):
    placed = (
        P("age", "lat", "lon"),
        P("age", "lat", "lon"),
        P("lat", "lon"),
        P("lat", "lon"),
        P("age"),
        P("age"),
        P("age"),
        P("age"),
        P(None, "age"),
        P(None, "lat", "lon"),
        P(None, "lat", "lon"),
        P("lat", "lon"),
        P("lat", "lon"),
        P("lat", "lon"),
        P(),
    )
    return jax.shard_map(
        local, mesh=mesh, in_specs=placed, out_specs=P("age", "lat", "lon"), check_vma=False
    )
```

```python
import functools

import jax
import jax.numpy as jnp
from jax import lax
from jax.experimental import pallas as pl
from jax.experimental.pallas import tpu as pltpu
from jax.sharding import PartitionSpec as P

ROWS, COLS = 64, 256
EROWS, ECOLS = ROWS + 8, COLS + 128
LANES = 128
N = 8
WIDE, NARROW = 4, 2
DENSITY, EAST, NORTH, SEA = 0, 32, 36, 40
ADJOINT, EFFORT, MASK, REGION, HABITAT = 44, 60, 76, 92, 94
STRIP = 96
PACKED = 2 * EROWS + 8
F32 = jnp.float32


def every_field(density, adjoint, effort, mask, east, north, region, sea, habitat):
    for c in range(N):
        yield density, c, DENSITY + WIDE * c, WIDE
    yield east, None, EAST, WIDE
    yield north, None, NORTH, WIDE
    yield sea, None, SEA, WIDE
    for c in range(N):
        yield adjoint, c, ADJOINT + NARROW * c, NARROW
    for f in range(N):
        yield effort, f, EFFORT + NARROW * f, NARROW
    for f in range(N):
        yield mask, f, MASK + NARROW * f, NARROW
    yield region, None, REGION, NARROW
    yield habitat, None, HABITAT, NARROW


def part(ref, index, rows, cols):
    block = ref[rows, cols] if index is None else ref[index, rows, cols]
    return block.astype(F32)


def lane_iota(rows):
    return lax.broadcasted_iota(jnp.int32, (rows, LANES), 1)


def turned(block, by):
    by = by % LANES
    return block if by == 0 else pltpu.roll(block, by, 1)


def pack_kernel(*refs):
    inputs, (to_east, to_west, to_north, to_south) = refs[:9], refs[9:]
    lane = lane_iota(ROWS)
    everything = slice(0, ROWS)
    right = jnp.zeros((ROWS, LANES), F32)
    left = jnp.zeros((ROWS, LANES), F32)
    for ref, index, place, width in every_field(*inputs):
        here = (lane >= place) & (lane < place + width)
        right = jnp.where(here, turned(part(ref, index, everything, slice(LANES, COLS)), place + width), right)
        left = jnp.where(here, turned(part(ref, index, everything, slice(0, LANES)), place), left)
        columns = slice(0, COLS)
        to_north[place : place + width, :] = part(ref, index, slice(ROWS - width, ROWS), columns)
        to_south[place : place + width, :] = part(ref, index, slice(0, width), columns)
    to_east[...] = right
    to_west[...] = left


def corner_kernel(north_in, south_in, west, east, to_north, to_south):
    if north_in is not to_north:
        to_north[0:STRIP, :] = north_in[0:STRIP, :]
        to_south[0:STRIP, :] = south_in[0:STRIP, :]
    to_north[STRIP : STRIP + 4, 0:LANES] = west[ROWS - 4 : ROWS, :]
    to_north[STRIP : STRIP + 4, LANES:COLS] = east[ROWS - 4 : ROWS, :]
    to_south[STRIP : STRIP + 4, 0:LANES] = west[0:4, :]
    to_south[STRIP : STRIP + 4, LANES:COLS] = east[0:4, :]
    to_north[STRIP + 4 :, :] = jnp.zeros((4, COLS), F32)
    to_south[STRIP + 4 :, :] = jnp.zeros((4, COLS), F32)


def at_all(out, slots, rows, value):
    for slot in range(slots):
        out[slot, rows, :] = value


def side_of(tile, k):
    return turned(tile, 4 * k + 2)


def packed_side(sides):
    lane = lane_iota(8)
    packed = jnp.zeros((8, LANES), F32)
    for k, side in enumerate(sides):
        packed = jnp.where((lane >= 4 * k) & (lane < 4 * k + 4), side_of(side, k), packed)
    return packed


def pack_into(out, index, x):
    out[index, 0:EROWS, :] = x[:, 0:LANES]
    out[index, EROWS : 2 * EROWS, :] = x[:, LANES:COLS]
    sides = [x[8 * k : 8 * k + 8, COLS:ECOLS] for k in range(EROWS // 8)]
    out[index, 2 * EROWS : PACKED, :] = packed_side(sides)


def unpack_into(out, packed):
    out[:, 0:LANES] = packed[0:EROWS]
    out[:, LANES:COLS] = packed[EROWS : 2 * EROWS]
    side = packed[2 * EROWS : PACKED]
    lane = lane_iota(8)
    here = (lane < NARROW) | (lane >= LANES - NARROW)
    for k in range(EROWS // 8):
        out[8 * k : 8 * k + 8, COLS:ECOLS] = jnp.where(here, turned(side, -(4 * k + 2)), 0.0)


def picked(received, keep):
    total = jnp.zeros((PACKED, LANES), F32)
    for slot in range(received.shape[0]):
        total = total + jnp.where(keep(slot), received[slot], 0.0)
    return total


def ahead(x, axis):
    return pltpu.roll(x, x.shape[axis] - 1, axis)


def behind(x, axis):
    return pltpu.roll(x, 1, axis)


def rates(flow):
    east, north = flow[0], flow[1]
    return jnp.maximum(-east, 0.0), jnp.maximum(east, 0.0), jnp.maximum(-north, 0.0), jnp.maximum(north, 0.0)


def moves(u):
    return ahead(u, 1), behind(u, 1), ahead(u, 0), behind(u, 0)


def spreading(u):
    e, w, n, s = moves(u)
    return ((e + w) + (n + s)) - 4.0 * u


def drifting(u, rate, out_rate):
    e, w, n, s = moves(u)
    return (rate[0] * e + rate[1] * w + rate[2] * n + rate[3] * s) - out_rate * u


def drifting_back(w, rate, out_rate):
    return (
        behind(rate[0] * w, 1) + ahead(rate[1] * w, 1) + behind(rate[2] * w, 0) + ahead(rate[3] * w, 0)
    ) - out_rate * w


def coeffs(flow, swim, spread):
    rate = rates(flow)
    to = [spread + swim * one for one in rate]
    return 1.0 - (to[0] + to[1] + to[2] + to[3]), *to


def advance(u, coefs, sea):
    centre, to_east, to_west, to_north, to_south = coefs
    e, w, n, s = moves(u)
    return sea * (centre * u + to_east * e + to_west * w + to_north * n + to_south * s)


def retreat(v, coefs):
    centre, to_east, to_west, to_north, to_south = coefs
    return (
        centre * v + behind(to_east * v, 1) + ahead(to_west * v, 1) + behind(to_north * v, 0) + ahead(to_south * v, 0)
    )


def strips(west_in, east_in, north_in, south_in, west, east):
    west[0:ROWS, :] = west_in[...]
    east[0:ROWS, :] = east_in[...]
    west[ROWS : ROWS + 4, :] = north_in[STRIP : STRIP + 4, 0:LANES]
    east[ROWS : ROWS + 4, :] = north_in[STRIP : STRIP + 4, LANES:COLS]
    west[ROWS + 4 : EROWS, :] = south_in[STRIP : STRIP + 4, 0:LANES]
    east[ROWS + 4 : EROWS, :] = south_in[STRIP : STRIP + 4, LANES:COLS]


def narrow_field(ref, index, place, west, east, north_in, south_in, out):
    width = NARROW
    core = part(ref, index, slice(0, ROWS), slice(0, COLS))
    for half in range(2):
        cols = slice(LANES * half, LANES * half + LANES)
        top = EROWS * half
        out[top : top + ROWS, :] = core[:, cols]
        out[top + ROWS : top + EROWS, :] = jnp.zeros((8, LANES), F32)
        out[top + ROWS : top + ROWS + width, :] = north_in[place : place + width, cols]
        out[top + EROWS - width : top + EROWS, :] = south_in[place : place + width, cols]
    lane = lane_iota(8)
    packed = jnp.zeros((8, LANES), F32)
    for k in range(EROWS // 8):
        rows = slice(8 * k, 8 * k + 8)
        here = (lane >= 4 * k) & (lane < 4 * k + width)
        packed = jnp.where(here, turned(west[rows, :], 4 * k - place), packed)
        here = (lane >= 4 * k + width) & (lane < 4 * k + 4)
        packed = jnp.where(here, turned(east[rows, :], 4 * k + width - place), packed)
    out[2 * EROWS : PACKED, :] = packed


def total_kernel(
    density, current_east, current_north, sea_mask, adjoint, west_in, east_in, north_in, south_in, swim, spread, mass,
    total_out, tail_out, density_out, flow_out, west, east,
):
    strips(west_in, east_in, north_in, south_in, west, east)
    narrow_field(adjoint, 0, ADJOINT, west, east, north_in, south_in, tail_out)
    lane = lane_iota(EROWS)
    wide = [(density, c, DENSITY + WIDE * c, density_out.at[c]) for c in range(N)]
    wide += [(current_east, None, EAST, flow_out.at[0]), (current_north, None, NORTH, flow_out.at[1])]
    wide += [(sea_mask, None, SEA, flow_out.at[2])]
    for ref, index, place, out in wide:
        out[0:ROWS, 0:COLS] = part(ref, index, slice(0, ROWS), slice(0, COLS))
        out[ROWS : ROWS + WIDE, 0:COLS] = north_in[place : place + WIDE, :]
        out[EROWS - WIDE : EROWS, 0:COLS] = south_in[place : place + WIDE, :]
        side = jnp.where(lane < WIDE, turned(east[...], -place), 0.0)
        side = jnp.where(lane >= LANES - WIDE, turned(west[...], LANES - WIDE - place), side)
        out[:, COLS:ECOLS] = side
    sums = [jnp.zeros((EROWS, ECOLS), F32) for _ in range(6)]
    for c in range(N):
        u, d, s = density_out[c], spread[c], swim[c]
        factors = (mass[c], mass[c] * d, mass[c] * s, mass[c] * d * d, mass[c] * d * s, mass[c] * s * s)
        sums = [total + factor * u for total, factor in zip(sums, factors, strict=True)]
    rate, sea = rates(flow_out), flow_out[2]
    out_rate = (rate[0] + rate[1]) + (rate[2] + rate[3])
    first = [
        sea * (sums[a] + spreading(sums[b]) + drifting(sums[c], rate, out_rate))
        for a, b, c in ((0, 1, 2), (1, 3, 4), (2, 4, 5))
    ]
    total = sea * (first[0] + spreading(first[1]) + drifting(first[2], rate, out_rate))
    slots = total_out.shape[0]
    at_all(total_out, slots, slice(0, EROWS), total[:, 0:LANES])
    at_all(total_out, slots, slice(EROWS, 2 * EROWS), total[:, LANES:COLS])
    sides = [total[8 * k : 8 * k + 8, COLS:ECOLS] for k in range(EROWS // 8)]
    at_all(total_out, slots, slice(2 * EROWS, PACKED), packed_side(sides))


def fleet_kernel(
    adjoint, effort, mask, region, habitat, west_in, east_in, north_in, south_in, density, flow,
    swim, spread, mortality, selectivity,
    settled_out, fishing_out, reported_out, region_out, carried_out, habitat_out, west, east, efforts,
):
    strips(west_in, east_in, north_in, south_in, west, east)

    def narrow(ref, index, place, out):
        narrow_field(ref, index, place, west, east, north_in, south_in, out)

    for k in range(N):
        narrow(adjoint, k, ADJOINT + NARROW * k, carried_out.at[k])
        narrow(effort, k, EFFORT + NARROW * k, efforts.at[k])
        narrow(mask, k, MASK + NARROW * k, reported_out.at[k])
    narrow(region, None, REGION, region_out)
    narrow(habitat, None, HABITAT, habitat_out)

    def tile(t, carry):
        rows = pl.ds(pl.multiple_of(t * 8, 8), 8)
        harvest = [efforts[f, rows, :] for f in range(N)]
        for f in range(N):
            reported_out[f, rows, :] = reported_out[f, rows, :] * harvest[f]
        for c in range(N):
            fishing = mortality[c] + selectivity[0, c] * harvest[0]
            for f in range(1, N):
                fishing = fishing + selectivity[f, c] * harvest[f]
            fishing_out[c, rows, :] = fishing
        return carry

    lax.fori_loop(0, PACKED // 8, tile, 0)

    def cohort(c, carry):
        coefs, sea = coeffs(flow, swim[c], spread[c]), flow[2]
        pack_into(settled_out, c, advance(advance(density[c], coefs, sea), coefs, sea))
        return carry

    lax.fori_loop(0, N, cohort, 0)


def catch_kernel(
    age, received, settled, fishing, reported, region, mass, selectivity, mort_out, catch_out, older, fleets
):
    shard = age[0]
    older[...] = picked(received, lambda slot: slot > shard)

    def pair(t, carry):
        places = [pl.ds(pl.multiple_of(t * 8, 8), 8), pl.ds(pl.multiple_of(EROWS + t * 8, 8), 8)]
        for rows in places:
            run = older[rows, :]
            taken = [jnp.zeros((8, LANES), F32) for _ in range(N)]
            for c in reversed(range(N)):
                total_mort = fishing[c, rows, :] + 0.02 * run
                mort_out[c, rows, :] = total_mort
                weighted = mass[c] * settled[c, rows, :]
                landed = weighted * ((1.0 - jnp.exp(-total_mort)) / total_mort)
                for f in range(N):
                    taken[f] = taken[f] + selectivity[f, c] * landed
                run = run + weighted
            for f in range(N):
                fleets[f, rows, :] = taken[f] * reported[f, rows, :]
        return carry

    lax.fori_loop(0, EROWS // 8, pair, 0)
    rows = slice(2 * EROWS, PACKED)
    run = older[rows, :]
    for c in reversed(range(N)):
        mort_out[c, rows, :] = fishing[c, rows, :] + 0.02 * run
        run = run + mass[c] * settled[c, rows, :]

    lane = lane_iota(N)
    fleet = lax.broadcasted_iota(jnp.int32, (N, LANES), 0)

    def one_region(r, table):
        sums = [jnp.zeros((8, LANES), F32) for _ in range(N)]
        for half in range(2):
            for t in range(ROWS // 8):
                rows = slice(EROWS * half + 8 * t, EROWS * half + 8 * t + 8)
                here = region[rows, :] == r.astype(F32)
                for f in range(N):
                    sums[f] = sums[f] + jnp.where(here, fleets[f, rows, :], 0.0)
        for f in range(N):
            column = jnp.sum(sums[f], axis=0, keepdims=True)
            column = jnp.sum(column, axis=1, keepdims=True)
            table = jnp.where((fleet == f) & (lane == r + 16 * f), column, table)
        return table

    table = lax.fori_loop(0, 16, one_region, jnp.zeros((N, LANES), F32))
    row = jnp.sum(table, axis=0, keepdims=True)
    catch_out[...] = jnp.broadcast_to(row, catch_out.shape)


def relay_kernel(catches, out):
    out[...] = jnp.broadcast_to(jnp.sum(catches[...], axis=0, keepdims=True), out.shape)


def slope_kernel(
    age, mort, settled, reported, carried, habitat, tail, mass, selectivity,
    still_out, reach_out, kept_out, yield_out, slope_out,
):
    last = age[0] == age[1] - 1

    def tile(t, carry):
        rows = pl.ds(pl.multiple_of(t * 8, 8), 8)
        still = jnp.zeros((8, LANES), F32)
        reach = [jnp.zeros((8, LANES), F32) for _ in range(N)]
        for c in range(N):
            total_mort, settled_c = mort[c, rows, :], settled[c, rows, :]
            survive = jnp.exp(-total_mort)
            yield_frac = (1.0 - survive) / total_mort
            if c + 1 < N:
                coming = carried[c + 1, rows, :]
            else:
                coming = jnp.where(last, carried[c, rows, :], tail[rows, :])
            kept = coming * habitat[rows, :] * survive
            slope = mass[c] * settled_c * (survive - yield_frac) / total_mort
            kept_out[c, rows, :] = kept
            yield_out[c, rows, :] = mass[c] * yield_frac
            slope_out[c, rows, :] = slope
            still = still - kept * settled_c
            for f in range(N):
                reach[f] = reach[f] + selectivity[f, c] * slope
        still_out[rows, :] = still
        for f in range(N):
            reach_out[f, rows, :] = reach[f] * reported[f, rows, :]
        return carry

    lax.fori_loop(0, PACKED // 8, tile, 0)


def press_kernel(catches, observed, region, still, reach, misfit_out, total_out, *, unit):
    predicted = jnp.sum(catches[...], axis=0, keepdims=True) * unit
    misfit = jnp.broadcast_to(1.0 - observed[...] / (1.0 + predicted), (8, LANES))
    misfit_out[...] = misfit
    for t in range(PACKED // 8):
        rows = slice(8 * t, 8 * t + 8)
        place = region[rows, :].astype(jnp.int32)
        total = still[rows, :]
        for f in range(N):
            total = total + jnp.take_along_axis(misfit, place + 16 * f, axis=1) * reach[f, rows, :]
        at_all(total_out, total_out.shape[0], rows, total)


def own_kernel(
    misfit_in, region, reported, settled, kept, yields, slope, flow, swim, spread, mass, selectivity,
    grad_out, bars, wide,
):
    misfit = misfit_in[...]

    def tile(t, carry):
        rows = pl.ds(pl.multiple_of(t * 8, 8), 8)
        place = region[rows, :].astype(jnp.int32)
        spread_back = [
            jnp.take_along_axis(misfit, place + 16 * f, axis=1) * reported[f, rows, :] for f in range(N)
        ]
        run = jnp.zeros((8, LANES), F32)
        for c in range(N):
            pull = selectivity[0, c] * spread_back[0]
            for f in range(1, N):
                pull = pull + selectivity[f, c] * spread_back[f]
            kept_c = kept[c, rows, :]
            bars[c, rows, :] = kept_c + yields[c, rows, :] * pull + (0.02 * mass[c]) * run
            run = run + (slope[c, rows, :] * pull - kept_c * settled[c, rows, :])
        return carry

    lax.fori_loop(0, PACKED // 8, tile, 0)

    def cohort(c, carry):
        coefs, sea = coeffs(flow, swim[c], spread[c]), flow[2]
        unpack_into(wide, bars[c])
        grad_out[c] = retreat(sea * retreat(sea * wide[...], coefs), coefs)[0:ROWS, 0:COLS]
        return carry

    lax.fori_loop(0, N, cohort, 0)


def final_kernel(age, received, own, flow, swim, spread, mass, grad_out, wide, basis):
    shard = age[0]
    unpack_into(wide, picked(received, lambda slot: slot < shard))
    rate, sea = rates(flow), flow[2]
    out_rate = (rate[0] + rate[1]) + (rate[2] + rate[3])
    plain = sea * wide[...]
    spread_once, drift_once = spreading(plain), drifting_back(plain, rate, out_rate)
    spread_sea, drift_sea = sea * spread_once, sea * drift_once
    fields = (
        plain,
        spread_sea + spread_once,
        drift_sea + drift_once,
        spreading(spread_sea),
        spreading(drift_sea) + drifting_back(spread_sea, rate, out_rate),
        drifting_back(drift_sea, rate, out_rate),
    )
    for k, field in enumerate(fields):
        basis[k] = field[0:ROWS, 0:COLS]
    for t in range(ROWS // 8):
        rows = slice(8 * t, 8 * t + 8)
        here = [basis[k, rows, :] for k in range(6)]
        for c in range(N):
            m, d, s = 0.02 * mass[c], spread[c], swim[c]
            younger = m * here[0] + (m * d) * here[1] + (m * s) * here[2]
            younger = younger + (m * d * d) * here[3] + (m * d * s) * here[4] + (m * s * s) * here[5]
            grad_out[c, rows, :] = own[c, rows, :] + younger


VMEM = pl.BlockSpec(memory_space=pltpu.VMEM)
SMEM = pl.BlockSpec(memory_space=pltpu.SMEM)


def shape(*dims):
    return pltpu.VMEM(dims, F32)


def far(*dims):
    return pltpu.HBM(dims, F32)


def near(x):
    return pltpu.with_memory_space_constraint(x, pltpu.VMEM)


def distant(*arrays):
    return [pltpu.with_memory_space_constraint(x, pltpu.HBM) for x in arrays]


def call(kernel, name, in_specs, outs, scratch=()):
    return pl.pallas_call(
        kernel,
        name=name,
        in_specs=in_specs,
        out_specs=[VMEM] * len(outs),
        out_shape=outs,
        scratch_shapes=[pltpu.VMEM(dims, F32) for dims in scratch],
        compiler_params=pltpu.CompilerParams(vmem_limit_bytes=24 << 20),
    )


def local(
    density, adjoint_next, current_east, current_north, swim_speed, diffusion, mortality, cohort_mass,
    selectivity, effort, catch_mask, region, sea_mask, habitat, observed,
):
    lons, lats, ages = (lax.axis_size(axis) for axis in ("lon", "lat", "age"))
    age = jnp.stack([lax.axis_index("age"), jnp.int32(ages)])
    inputs = distant(
        density, adjoint_next, effort, catch_mask, current_east, current_north, region, sea_mask, habitat
    )
    density, adjoint_next, effort, catch_mask, current_east, current_north, region, sea_mask, habitat = inputs
    strip_rows = STRIP + 8

    to_east, to_west, to_north, to_south = call(
        pack_kernel,
        "pack",
        [VMEM] * 9,
        [shape(ROWS, LANES), shape(ROWS, LANES), shape(strip_rows, COLS), shape(strip_rows, COLS)],
    )(*inputs)
    from_west = near(lax.ppermute(to_east, "lon", [(i, (i + 1) % lons) for i in range(lons)]))
    from_east = near(lax.ppermute(to_west, "lon", [((i + 1) % lons, i) for i in range(lons)]))
    to_north, to_south = pl.pallas_call(
        corner_kernel,
        name="corner",
        in_specs=[VMEM] * 4,
        out_specs=[VMEM, VMEM],
        out_shape=[shape(strip_rows, COLS)] * 2,
        input_output_aliases={0: 0, 1: 1},
        compiler_params=pltpu.CompilerParams(vmem_limit_bytes=4 << 20),
    )(near(to_north), near(to_south), from_west, from_east)
    from_south = near(lax.ppermute(to_north, "lat", [(i, i + 1) for i in range(lats - 1)]))
    from_north = near(lax.ppermute(to_south, "lat", [(i + 1, i) for i in range(lats - 1)]))
    halos = (from_west, from_east, from_north, from_south)

    packed = (PACKED, LANES)
    extended = (EROWS, ECOLS)
    totals, tail, density_ext, flow = call(
        total_kernel,
        "total",
        [VMEM] * 9 + [SMEM] * 3,
        [shape(ages, *packed), shape(*packed), shape(N, *extended), far(3, *extended)],
        [(EROWS, LANES), (EROWS, LANES)],
    )(density, current_east, current_north, sea_mask, adjoint_next, *halos, swim_speed, diffusion, cohort_mass)
    totals = lax.all_to_all(totals, "age", 0, 0, tiled=True)
    tail = lax.ppermute(tail, "age", [(i + 1, i) for i in range(ages - 1)])

    settled, fishing, reported, regions, carried, habitats = call(
        fleet_kernel,
        "fleet",
        [VMEM] * 11 + [SMEM] * 4,
        [shape(N, *packed)] * 3 + [shape(*packed), far(N, *packed), far(*packed)],
        [(EROWS, LANES), (EROWS, LANES), (N, *packed)],
    )(
        adjoint_next, effort, catch_mask, region, habitat, *halos, near(density_ext), *distant(flow),
        swim_speed, diffusion, mortality, selectivity,
    )
    settled, reported, regions = near(settled), near(reported), near(regions)

    mort, catches = call(
        catch_kernel,
        "catch",
        [SMEM] + [VMEM] * 5 + [SMEM] * 2,
        [shape(N, *packed), shape(lons, LANES)],
        [packed, (N, *packed)],
    )(age, near(totals), settled, near(fishing), reported, regions, cohort_mass, selectivity)
    catches = near(lax.all_to_all(catches, "lon", 0, 0, tiled=True))
    (catches,) = call(relay_kernel, "relay", [VMEM], [shape(lats * ages, LANES)])(catches)
    catches = near(lax.all_to_all(catches, ("lat", "age"), 0, 0, tiled=True))

    still, reach, kept, yields, slope = call(
        slope_kernel,
        "slope",
        [SMEM] + [VMEM] * 6 + [SMEM] * 2,
        [shape(*packed), shape(N, *packed)] + [far(N, *packed)] * 3,
    )(age, near(mort), settled, reported, *distant(carried, habitats), near(tail), cohort_mass, selectivity)

    unit = observed.shape[1] / (ROWS * COLS * lons * lats)
    misfit, totals = call(
        functools.partial(press_kernel, unit=unit),
        "press",
        [VMEM] * 5,
        [shape(8, LANES), shape(ages, *packed)],
    )(catches, observed.reshape(1, LANES), regions, near(still), near(reach))
    totals = lax.all_to_all(totals, "age", 0, 0, tiled=True)

    kept, yields, slope, flow = distant(kept, yields, slope, flow)
    (own,) = call(
        own_kernel,
        "own",
        [VMEM] * 8 + [SMEM] * 4,
        [shape(N, ROWS, COLS)],
        [(N, *packed), extended],
    )(near(misfit), regions, reported, settled, kept, yields, slope, flow, swim_speed, diffusion, cohort_mass, selectivity)
    (grad,) = call(
        final_kernel,
        "final",
        [SMEM] + [VMEM] * 3 + [SMEM] * 3,
        [far(N, ROWS, COLS)],
        [extended, (6, ROWS, COLS)],
    )(age, near(totals), near(own), flow, swim_speed, diffusion, cohort_mass)
    return grad


def solution(mesh):
    placed = (
        P("age", "lat", "lon"),
        P("age", "lat", "lon"),
        P("lat", "lon"),
        P("lat", "lon"),
        P("age"),
        P("age"),
        P("age"),
        P("age"),
        P(None, "age"),
        P(None, "lat", "lon"),
        P(None, "lat", "lon"),
        P("lat", "lon"),
        P("lat", "lon"),
        P("lat", "lon"),
        P(),
    )
    return jax.shard_map(
        local, mesh=mesh, in_specs=placed, out_specs=P("age", "lat", "lon"), check_vma=False
    )
```

```python
import functools

import jax
import jax.numpy as jnp
from jax import lax
from jax.experimental import pallas as pl
from jax.experimental.pallas import tpu as pltpu
from jax.sharding import PartitionSpec as P

ROWS, COLS = 64, 256
EROWS, ECOLS = ROWS + 8, COLS + 128
LANES = 128
N = 8
WIDE, NARROW = 4, 2
DENSITY, EAST, NORTH, SEA = 0, 32, 36, 40
ADJOINT, EFFORT, MASK, REGION, HABITAT = 44, 60, 76, 92, 94
STRIP = 96
PACKED = 2 * EROWS + 8
F32 = jnp.float32


def every_field(density, adjoint, effort, mask, east, north, region, sea, habitat):
    for c in range(N):
        yield density, c, DENSITY + WIDE * c, WIDE
    yield east, None, EAST, WIDE
    yield north, None, NORTH, WIDE
    yield sea, None, SEA, WIDE
    for c in range(N):
        yield adjoint, c, ADJOINT + NARROW * c, NARROW
    for f in range(N):
        yield effort, f, EFFORT + NARROW * f, NARROW
    for f in range(N):
        yield mask, f, MASK + NARROW * f, NARROW
    yield region, None, REGION, NARROW
    yield habitat, None, HABITAT, NARROW


def part(ref, index, rows, cols):
    block = ref[rows, cols] if index is None else ref[index, rows, cols]
    return block.astype(F32)


def lane_iota(rows):
    return lax.broadcasted_iota(jnp.int32, (rows, LANES), 1)


def turned(block, by):
    by = by % LANES
    return block if by == 0 else pltpu.roll(block, by, 1)


def pack_kernel(*refs):
    inputs, (to_east, to_west, to_north, to_south) = refs[:9], refs[9:]
    lane = lane_iota(ROWS)
    everything = slice(0, ROWS)
    right = jnp.zeros((ROWS, LANES), F32)
    left = jnp.zeros((ROWS, LANES), F32)
    for ref, index, place, width in every_field(*inputs):
        here = (lane >= place) & (lane < place + width)
        right = jnp.where(here, turned(part(ref, index, everything, slice(LANES, COLS)), place + width), right)
        left = jnp.where(here, turned(part(ref, index, everything, slice(0, LANES)), place), left)
        columns = slice(0, COLS)
        to_north[place : place + width, :] = part(ref, index, slice(ROWS - width, ROWS), columns)
        to_south[place : place + width, :] = part(ref, index, slice(0, width), columns)
    to_east[...] = right
    to_west[...] = left


def corner_kernel(north_in, south_in, west, east, to_north, to_south):
    if north_in is not to_north:
        to_north[0:STRIP, :] = north_in[0:STRIP, :]
        to_south[0:STRIP, :] = south_in[0:STRIP, :]
    to_north[STRIP : STRIP + 4, 0:LANES] = west[ROWS - 4 : ROWS, :]
    to_north[STRIP : STRIP + 4, LANES:COLS] = east[ROWS - 4 : ROWS, :]
    to_south[STRIP : STRIP + 4, 0:LANES] = west[0:4, :]
    to_south[STRIP : STRIP + 4, LANES:COLS] = east[0:4, :]
    to_north[STRIP + 4 :, :] = jnp.zeros((4, COLS), F32)
    to_south[STRIP + 4 :, :] = jnp.zeros((4, COLS), F32)


def at_all(out, slots, rows, value):
    for slot in range(slots):
        out[slot, rows, :] = value


def side_of(tile, k):
    return turned(tile, 4 * k + 2)


def packed_side(sides):
    lane = lane_iota(8)
    packed = jnp.zeros((8, LANES), F32)
    for k, side in enumerate(sides):
        packed = jnp.where((lane >= 4 * k) & (lane < 4 * k + 4), side_of(side, k), packed)
    return packed


def pack_into(out, index, x):
    out[index, 0:EROWS, :] = x[:, 0:LANES]
    out[index, EROWS : 2 * EROWS, :] = x[:, LANES:COLS]
    sides = [x[8 * k : 8 * k + 8, COLS:ECOLS] for k in range(EROWS // 8)]
    out[index, 2 * EROWS : PACKED, :] = packed_side(sides)


def unpack_into(out, packed):
    out[:, 0:LANES] = packed[0:EROWS]
    out[:, LANES:COLS] = packed[EROWS : 2 * EROWS]
    side = packed[2 * EROWS : PACKED]
    lane = lane_iota(8)
    here = (lane < NARROW) | (lane >= LANES - NARROW)
    for k in range(EROWS // 8):
        out[8 * k : 8 * k + 8, COLS:ECOLS] = jnp.where(here, turned(side, -(4 * k + 2)), 0.0)


def picked(received, keep):
    total = jnp.zeros((PACKED, LANES), F32)
    for slot in range(received.shape[0]):
        total = total + jnp.where(keep(slot), received[slot], 0.0)
    return total


def ahead(x, axis):
    return pltpu.roll(x, x.shape[axis] - 1, axis)


def behind(x, axis):
    return pltpu.roll(x, 1, axis)


def rates(flow):
    east, north = flow[0], flow[1]
    return jnp.maximum(-east, 0.0), jnp.maximum(east, 0.0), jnp.maximum(-north, 0.0), jnp.maximum(north, 0.0)


def moves(u):
    return ahead(u, 1), behind(u, 1), ahead(u, 0), behind(u, 0)


def spreading(u):
    e, w, n, s = moves(u)
    return ((e + w) + (n + s)) - 4.0 * u


def drifting(u, rate, out_rate):
    e, w, n, s = moves(u)
    return (rate[0] * e + rate[1] * w + rate[2] * n + rate[3] * s) - out_rate * u


def drifting_back(w, rate, out_rate):
    return (
        behind(rate[0] * w, 1) + ahead(rate[1] * w, 1) + behind(rate[2] * w, 0) + ahead(rate[3] * w, 0)
    ) - out_rate * w


def coeffs(flow, swim, spread):
    rate = rates(flow)
    to = [spread + swim * one for one in rate]
    return 1.0 - (to[0] + to[1] + to[2] + to[3]), *to


def advance(u, coefs, sea):
    centre, to_east, to_west, to_north, to_south = coefs
    e, w, n, s = moves(u)
    return sea * (centre * u + to_east * e + to_west * w + to_north * n + to_south * s)


def retreat(v, coefs):
    centre, to_east, to_west, to_north, to_south = coefs
    return (
        centre * v + behind(to_east * v, 1) + ahead(to_west * v, 1) + behind(to_north * v, 0) + ahead(to_south * v, 0)
    )


def strips(west_in, east_in, north_in, south_in, west, east):
    west[0:ROWS, :] = west_in[...]
    east[0:ROWS, :] = east_in[...]
    west[ROWS : ROWS + 4, :] = north_in[STRIP : STRIP + 4, 0:LANES]
    east[ROWS : ROWS + 4, :] = north_in[STRIP : STRIP + 4, LANES:COLS]
    west[ROWS + 4 : EROWS, :] = south_in[STRIP : STRIP + 4, 0:LANES]
    east[ROWS + 4 : EROWS, :] = south_in[STRIP : STRIP + 4, LANES:COLS]


def narrow_field(ref, index, place, west, east, north_in, south_in, out):
    width = NARROW
    core = part(ref, index, slice(0, ROWS), slice(0, COLS))
    for half in range(2):
        cols = slice(LANES * half, LANES * half + LANES)
        top = EROWS * half
        out[top : top + ROWS, :] = core[:, cols]
        out[top + ROWS : top + EROWS, :] = jnp.zeros((8, LANES), F32)
        out[top + ROWS : top + ROWS + width, :] = north_in[place : place + width, cols]
        out[top + EROWS - width : top + EROWS, :] = south_in[place : place + width, cols]
    lane = lane_iota(8)
    packed = jnp.zeros((8, LANES), F32)
    for k in range(EROWS // 8):
        rows = slice(8 * k, 8 * k + 8)
        here = (lane >= 4 * k) & (lane < 4 * k + width)
        packed = jnp.where(here, turned(west[rows, :], 4 * k - place), packed)
        here = (lane >= 4 * k + width) & (lane < 4 * k + 4)
        packed = jnp.where(here, turned(east[rows, :], 4 * k + width - place), packed)
    out[2 * EROWS : PACKED, :] = packed


def total_kernel(
    density, current_east, current_north, sea_mask, adjoint, west_in, east_in, north_in, south_in, swim, spread, mass,
    total_out, tail_out, density_out, flow_out, west, east,
):
    strips(west_in, east_in, north_in, south_in, west, east)
    narrow_field(adjoint, 0, ADJOINT, west, east, north_in, south_in, tail_out)
    lane = lane_iota(EROWS)
    wide = [(density, c, DENSITY + WIDE * c, density_out.at[c]) for c in range(N)]
    wide += [(current_east, None, EAST, flow_out.at[0]), (current_north, None, NORTH, flow_out.at[1])]
    wide += [(sea_mask, None, SEA, flow_out.at[2])]
    for ref, index, place, out in wide:
        out[0:ROWS, 0:COLS] = part(ref, index, slice(0, ROWS), slice(0, COLS))
        out[ROWS : ROWS + WIDE, 0:COLS] = north_in[place : place + WIDE, :]
        out[EROWS - WIDE : EROWS, 0:COLS] = south_in[place : place + WIDE, :]
        side = jnp.where(lane < WIDE, turned(east[...], -place), 0.0)
        side = jnp.where(lane >= LANES - WIDE, turned(west[...], LANES - WIDE - place), side)
        out[:, COLS:ECOLS] = side
    sums = [jnp.zeros((EROWS, ECOLS), F32) for _ in range(6)]
    for c in range(N):
        u, d, s = density_out[c], spread[c], swim[c]
        factors = (mass[c], mass[c] * d, mass[c] * s, mass[c] * d * d, mass[c] * d * s, mass[c] * s * s)
        sums = [total + factor * u for total, factor in zip(sums, factors, strict=True)]
    rate, sea = rates(flow_out), flow_out[2]
    out_rate = (rate[0] + rate[1]) + (rate[2] + rate[3])
    first = [
        sea * (sums[a] + spreading(sums[b]) + drifting(sums[c], rate, out_rate))
        for a, b, c in ((0, 1, 2), (1, 3, 4), (2, 4, 5))
    ]
    total = sea * (first[0] + spreading(first[1]) + drifting(first[2], rate, out_rate))
    slots = total_out.shape[0]
    at_all(total_out, slots, slice(0, EROWS), total[:, 0:LANES])
    at_all(total_out, slots, slice(EROWS, 2 * EROWS), total[:, LANES:COLS])
    sides = [total[8 * k : 8 * k + 8, COLS:ECOLS] for k in range(EROWS // 8)]
    at_all(total_out, slots, slice(2 * EROWS, PACKED), packed_side(sides))


def fleet_kernel(
    adjoint, effort, mask, region, habitat, west_in, east_in, north_in, south_in, density, flow,
    swim, spread, mortality, selectivity,
    settled_out, fishing_out, reported_out, region_out, carried_out, habitat_out, west, east, efforts,
):
    strips(west_in, east_in, north_in, south_in, west, east)

    def narrow(ref, index, place, out):
        narrow_field(ref, index, place, west, east, north_in, south_in, out)

    for k in range(N):
        narrow(adjoint, k, ADJOINT + NARROW * k, carried_out.at[k])
        narrow(effort, k, EFFORT + NARROW * k, efforts.at[k])
        narrow(mask, k, MASK + NARROW * k, reported_out.at[k])
    narrow(region, None, REGION, region_out)
    narrow(habitat, None, HABITAT, habitat_out)

    def tile(t, carry):
        rows = pl.ds(pl.multiple_of(t * 8, 8), 8)
        harvest = [efforts[f, rows, :] for f in range(N)]
        for f in range(N):
            reported_out[f, rows, :] = reported_out[f, rows, :] * harvest[f]
        for c in range(N):
            fishing = mortality[c] + selectivity[0, c] * harvest[0]
            for f in range(1, N):
                fishing = fishing + selectivity[f, c] * harvest[f]
            fishing_out[c, rows, :] = fishing
        return carry

    lax.fori_loop(0, PACKED // 8, tile, 0)

    def cohort(c, carry):
        coefs, sea = coeffs(flow, swim[c], spread[c]), flow[2]
        pack_into(settled_out, c, advance(advance(density[c], coefs, sea), coefs, sea))
        return carry

    lax.fori_loop(0, N, cohort, 0)


def catch_kernel(
    age, received, settled, fishing, reported, region, mass, selectivity, mort_out, catch_out, older, fleets
):
    shard = age[0]
    older[...] = picked(received, lambda slot: slot > shard)

    def pair(t, carry):
        places = [pl.ds(pl.multiple_of(t * 8, 8), 8), pl.ds(pl.multiple_of(EROWS + t * 8, 8), 8)]
        for rows in places:
            run = older[rows, :]
            taken = [jnp.zeros((8, LANES), F32) for _ in range(N)]
            for c in reversed(range(N)):
                total_mort = fishing[c, rows, :] + 0.02 * run
                mort_out[c, rows, :] = total_mort
                weighted = mass[c] * settled[c, rows, :]
                landed = weighted * ((1.0 - jnp.exp(-total_mort)) / total_mort)
                for f in range(N):
                    taken[f] = taken[f] + selectivity[f, c] * landed
                run = run + weighted
            for f in range(N):
                fleets[f, rows, :] = taken[f] * reported[f, rows, :]
        return carry

    lax.fori_loop(0, EROWS // 8, pair, 0)
    rows = slice(2 * EROWS, PACKED)
    run = older[rows, :]
    for c in reversed(range(N)):
        mort_out[c, rows, :] = fishing[c, rows, :] + 0.02 * run
        run = run + mass[c] * settled[c, rows, :]

    lane = lane_iota(N)
    fleet = lax.broadcasted_iota(jnp.int32, (N, LANES), 0)

    def one_region(r, table):
        sums = [jnp.zeros((8, LANES), F32) for _ in range(N)]
        for half in range(2):
            for t in range(ROWS // 8):
                rows = slice(EROWS * half + 8 * t, EROWS * half + 8 * t + 8)
                here = region[rows, :] == r.astype(F32)
                for f in range(N):
                    sums[f] = sums[f] + jnp.where(here, fleets[f, rows, :], 0.0)
        for f in range(N):
            column = jnp.sum(sums[f], axis=0, keepdims=True)
            column = jnp.sum(column, axis=1, keepdims=True)
            table = jnp.where((fleet == f) & (lane == r + 16 * f), column, table)
        return table

    table = lax.fori_loop(0, 16, one_region, jnp.zeros((N, LANES), F32))
    row = jnp.sum(table, axis=0, keepdims=True)
    catch_out[...] = jnp.broadcast_to(row, catch_out.shape)


def relay_kernel(catches, out):
    out[...] = jnp.broadcast_to(jnp.sum(catches[...], axis=0, keepdims=True), out.shape)


def slope_kernel(
    age, mort, settled, reported, carried, habitat, tail, mass, selectivity,
    still_out, reach_out, kept_out, yield_out, slope_out,
):
    last = age[0] == age[1] - 1

    def tile(t, carry):
        rows = pl.ds(pl.multiple_of(t * 8, 8), 8)
        still = jnp.zeros((8, LANES), F32)
        reach = [jnp.zeros((8, LANES), F32) for _ in range(N)]
        for c in range(N):
            total_mort, settled_c = mort[c, rows, :], settled[c, rows, :]
            survive = jnp.exp(-total_mort)
            yield_frac = (1.0 - survive) / total_mort
            if c + 1 < N:
                coming = carried[c + 1, rows, :]
            else:
                coming = jnp.where(last, carried[c, rows, :], tail[rows, :])
            kept = coming * habitat[rows, :] * survive
            slope = mass[c] * settled_c * (survive - yield_frac) / total_mort
            kept_out[c, rows, :] = kept
            yield_out[c, rows, :] = mass[c] * yield_frac
            slope_out[c, rows, :] = slope
            still = still - kept * settled_c
            for f in range(N):
                reach[f] = reach[f] + selectivity[f, c] * slope
        still_out[rows, :] = still
        for f in range(N):
            reach_out[f, rows, :] = reach[f] * reported[f, rows, :]
        return carry

    lax.fori_loop(0, PACKED // 8, tile, 0)


def press_kernel(catches, observed, region, still, reach, misfit_out, total_out, *, unit):
    predicted = jnp.sum(catches[...], axis=0, keepdims=True) * unit
    misfit = jnp.broadcast_to(1.0 - observed[...] / (1.0 + predicted), (8, LANES))
    misfit_out[...] = misfit
    for t in range(PACKED // 8):
        rows = slice(8 * t, 8 * t + 8)
        place = region[rows, :].astype(jnp.int32)
        total = still[rows, :]
        for f in range(N):
            total = total + jnp.take_along_axis(misfit, place + 16 * f, axis=1) * reach[f, rows, :]
        at_all(total_out, total_out.shape[0], rows, total)


def own_kernel(
    misfit_in, region, reported, settled, kept, yields, slope, flow, swim, spread, mass, selectivity,
    grad_out, bars, wide,
):
    misfit = misfit_in[...]

    def tile(t, carry):
        rows = pl.ds(pl.multiple_of(t * 8, 8), 8)
        place = region[rows, :].astype(jnp.int32)
        spread_back = [
            jnp.take_along_axis(misfit, place + 16 * f, axis=1) * reported[f, rows, :] for f in range(N)
        ]
        run = jnp.zeros((8, LANES), F32)
        for c in range(N):
            pull = selectivity[0, c] * spread_back[0]
            for f in range(1, N):
                pull = pull + selectivity[f, c] * spread_back[f]
            kept_c = kept[c, rows, :]
            bars[c, rows, :] = kept_c + yields[c, rows, :] * pull + (0.02 * mass[c]) * run
            run = run + (slope[c, rows, :] * pull - kept_c * settled[c, rows, :])
        return carry

    lax.fori_loop(0, PACKED // 8, tile, 0)

    def cohort(c, carry):
        coefs, sea = coeffs(flow, swim[c], spread[c]), flow[2]
        unpack_into(wide, bars[c])
        grad_out[c] = retreat(sea * retreat(sea * wide[...], coefs), coefs)[0:ROWS, 0:COLS]
        return carry

    lax.fori_loop(0, N, cohort, 0)


def final_kernel(age, received, own, flow, swim, spread, mass, grad_out, wide, basis):
    shard = age[0]
    unpack_into(wide, picked(received, lambda slot: slot < shard))
    rate, sea = rates(flow), flow[2]
    out_rate = (rate[0] + rate[1]) + (rate[2] + rate[3])
    plain = sea * wide[...]
    spread_once, drift_once = spreading(plain), drifting_back(plain, rate, out_rate)
    spread_sea, drift_sea = sea * spread_once, sea * drift_once
    fields = (
        plain,
        spread_sea + spread_once,
        drift_sea + drift_once,
        spreading(spread_sea),
        spreading(drift_sea) + drifting_back(spread_sea, rate, out_rate),
        drifting_back(drift_sea, rate, out_rate),
    )
    for k, field in enumerate(fields):
        basis[k] = field[0:ROWS, 0:COLS]
    for t in range(ROWS // 8):
        rows = slice(8 * t, 8 * t + 8)
        here = [basis[k, rows, :] for k in range(6)]
        for c in range(N):
            m, d, s = 0.02 * mass[c], spread[c], swim[c]
            younger = m * here[0] + (m * d) * here[1] + (m * s) * here[2]
            younger = younger + (m * d * d) * here[3] + (m * d * s) * here[4] + (m * s * s) * here[5]
            grad_out[c, rows, :] = own[c, rows, :] + younger


VMEM = pl.BlockSpec(memory_space=pltpu.VMEM)
SMEM = pl.BlockSpec(memory_space=pltpu.SMEM)


def shape(*dims):
    return pltpu.VMEM(dims, F32)


def far(*dims):
    return pltpu.HBM(dims, F32)


def near(x):
    return pltpu.with_memory_space_constraint(x, pltpu.VMEM)


def distant(*arrays):
    return [pltpu.with_memory_space_constraint(x, pltpu.HBM) for x in arrays]


def call(kernel, name, in_specs, outs, scratch=()):
    return pl.pallas_call(
        kernel,
        name=name,
        in_specs=in_specs,
        out_specs=[VMEM] * len(outs),
        out_shape=outs,
        scratch_shapes=[pltpu.VMEM(dims, F32) for dims in scratch],
        compiler_params=pltpu.CompilerParams(vmem_limit_bytes=24 << 20),
    )


def local(
    density, adjoint_next, current_east, current_north, swim_speed, diffusion, mortality, cohort_mass,
    selectivity, effort, catch_mask, region, sea_mask, habitat, observed,
):
    lons, lats, ages = (lax.axis_size(axis) for axis in ("lon", "lat", "age"))
    age = jnp.stack([lax.axis_index("age"), jnp.int32(ages)])
    inputs = distant(
        density, adjoint_next, effort, catch_mask, current_east, current_north, region, sea_mask, habitat
    )
    density, adjoint_next, effort, catch_mask, current_east, current_north, region, sea_mask, habitat = inputs
    strip_rows = STRIP + 8

    to_east, to_west, to_north, to_south = call(
        pack_kernel,
        "pack",
        [VMEM] * 9,
        [shape(ROWS, LANES), shape(ROWS, LANES), shape(strip_rows, COLS), shape(strip_rows, COLS)],
    )(*inputs)
    from_west = lax.ppermute(to_east, "lon", [(i, (i + 1) % lons) for i in range(lons)])
    from_east = lax.ppermute(to_west, "lon", [((i + 1) % lons, i) for i in range(lons)])
    to_north, to_south = pl.pallas_call(
        corner_kernel,
        name="corner",
        in_specs=[VMEM] * 4,
        out_specs=[VMEM, VMEM],
        out_shape=[shape(strip_rows, COLS)] * 2,
        input_output_aliases={0: 0, 1: 1},
        compiler_params=pltpu.CompilerParams(vmem_limit_bytes=4 << 20),
    )(near(to_north), near(to_south), near(from_west), near(from_east))
    from_south = lax.ppermute(to_north, "lat", [(i, i + 1) for i in range(lats - 1)])
    from_north = lax.ppermute(to_south, "lat", [(i + 1, i) for i in range(lats - 1)])
    halos = (from_west, from_east, from_north, from_south)

    packed = (PACKED, LANES)
    extended = (EROWS, ECOLS)
    totals, tail, density_ext, flow = call(
        total_kernel,
        "total",
        [VMEM] * 9 + [SMEM] * 3,
        [shape(ages, *packed), shape(*packed), shape(N, *extended), far(3, *extended)],
        [(EROWS, LANES), (EROWS, LANES)],
    )(density, current_east, current_north, sea_mask, adjoint_next, *map(near, halos), swim_speed, diffusion, cohort_mass)
    totals = lax.all_to_all(totals, "age", 0, 0, tiled=True)
    tail = lax.ppermute(tail, "age", [(i + 1, i) for i in range(ages - 1)])

    settled, fishing, reported, regions, carried, habitats = call(
        fleet_kernel,
        "fleet",
        [VMEM] * 11 + [SMEM] * 4,
        [shape(N, *packed)] * 3 + [shape(*packed), far(N, *packed), far(*packed)],
        [(EROWS, LANES), (EROWS, LANES), (N, *packed)],
    )(
        adjoint_next, effort, catch_mask, region, habitat, *distant(*halos), near(density_ext), *distant(flow),
        swim_speed, diffusion, mortality, selectivity,
    )
    settled, reported, regions = near(settled), near(reported), near(regions)

    mort, catches = call(
        catch_kernel,
        "catch",
        [SMEM] + [VMEM] * 5 + [SMEM] * 2,
        [shape(N, *packed), shape(ages, LANES)],
        [packed, (N, *packed)],
    )(age, near(totals), settled, near(fishing), reported, regions, cohort_mass, selectivity)
    catches = near(lax.all_to_all(catches, "age", 0, 0, tiled=True))
    (catches,) = call(relay_kernel, "relay", [VMEM], [shape(lons * lats, LANES)])(catches)
    catches = near(lax.all_to_all(catches, ("lon", "lat"), 0, 0, tiled=True))

    still, reach, kept, yields, slope = call(
        slope_kernel,
        "slope",
        [SMEM] + [VMEM] * 6 + [SMEM] * 2,
        [shape(*packed), shape(N, *packed)] + [far(N, *packed)] * 3,
    )(age, near(mort), settled, reported, *distant(carried, habitats), near(tail), cohort_mass, selectivity)

    unit = observed.shape[1] / (ROWS * COLS * lons * lats)
    misfit, totals = call(
        functools.partial(press_kernel, unit=unit),
        "press",
        [VMEM] * 5,
        [shape(8, LANES), shape(ages, *packed)],
    )(catches, observed.reshape(1, LANES), regions, near(still), near(reach))
    totals = lax.all_to_all(totals, "age", 0, 0, tiled=True)

    kept, yields, slope, flow = distant(kept, yields, slope, flow)
    (own,) = call(
        own_kernel,
        "own",
        [VMEM] * 8 + [SMEM] * 4,
        [shape(N, ROWS, COLS)],
        [(N, *packed), extended],
    )(near(misfit), regions, reported, settled, kept, yields, slope, flow, swim_speed, diffusion, cohort_mass, selectivity)
    (grad,) = call(
        final_kernel,
        "final",
        [SMEM] + [VMEM] * 3 + [SMEM] * 3,
        [far(N, ROWS, COLS)],
        [extended, (6, ROWS, COLS)],
    )(age, near(totals), near(own), flow, swim_speed, diffusion, cohort_mass)
    return grad


def solution(mesh):
    placed = (
        P("age", "lat", "lon"),
        P("age", "lat", "lon"),
        P("lat", "lon"),
        P("lat", "lon"),
        P("age"),
        P("age"),
        P("age"),
        P("age"),
        P(None, "age"),
        P(None, "lat", "lon"),
        P(None, "lat", "lon"),
        P("lat", "lon"),
        P("lat", "lon"),
        P("lat", "lon"),
        P(),
    )
    return jax.shard_map(
        local, mesh=mesh, in_specs=placed, out_specs=P("age", "lat", "lon"), check_vma=False
    )
```

```python
import functools

import jax
import jax.numpy as jnp
from jax import lax
from jax.experimental import pallas as pl
from jax.experimental.pallas import tpu as pltpu
from jax.sharding import PartitionSpec as P


ROWS, COLS = 64, 256
EROWS, ECOLS = ROWS + 8, COLS + 128
LANES = 128
N = 8
WIDE, NARROW = 4, 2
DENSITY, EAST, NORTH, SEA = 0, 32, 36, 40
ADJOINT, EFFORT, MASK, REGION, HABITAT = 44, 60, 76, 92, 94
STRIP = 96
PACKED = 2 * EROWS + 8
F32 = jnp.float32
SEPARATE = False


def every_field(density, adjoint, effort, mask, east, north, region, sea, habitat):
    for c in range(N):
        yield density, c, DENSITY + WIDE * c, WIDE
    yield east, None, EAST, WIDE
    yield north, None, NORTH, WIDE
    yield sea, None, SEA, WIDE
    for c in range(N):
        yield adjoint, c, ADJOINT + NARROW * c, NARROW
    for f in range(N):
        yield effort, f, EFFORT + NARROW * f, NARROW
    for f in range(N):
        yield mask, f, MASK + NARROW * f, NARROW
    yield region, None, REGION, NARROW
    yield habitat, None, HABITAT, NARROW


def part(ref, index, rows, cols):
    block = ref[rows, cols] if index is None else ref[index, rows, cols]
    return block.astype(F32)


def lane_iota(rows):
    return lax.broadcasted_iota(jnp.int32, (rows, LANES), 1)


def turned(block, by):
    by = by % LANES
    return block if by == 0 else pltpu.roll(block, by, 1)


def pack_kernel(*refs):
    inputs, (to_east, to_west, to_north, to_south) = refs[:9], refs[9:]
    lane = lane_iota(ROWS)
    everything = slice(0, ROWS)
    right = jnp.zeros((ROWS, LANES), F32)
    left = jnp.zeros((ROWS, LANES), F32)
    for ref, index, place, width in every_field(*inputs):
        here = (lane >= place) & (lane < place + width)
        right = jnp.where(here, turned(part(ref, index, everything, slice(LANES, COLS)), place + width), right)
        left = jnp.where(here, turned(part(ref, index, everything, slice(0, LANES)), place), left)
        columns = slice(0, COLS)
        to_north[place : place + width, :] = part(ref, index, slice(ROWS - width, ROWS), columns)
        to_south[place : place + width, :] = part(ref, index, slice(0, width), columns)
    to_east[...] = right
    to_west[...] = left


def corner_kernel(north_in, south_in, west, east, to_north, to_south):
    if north_in is not to_north:
        to_north[0:STRIP, :] = north_in[0:STRIP, :]
        to_south[0:STRIP, :] = south_in[0:STRIP, :]
    to_north[STRIP : STRIP + 4, 0:LANES] = west[ROWS - 4 : ROWS, :]
    to_north[STRIP : STRIP + 4, LANES:COLS] = east[ROWS - 4 : ROWS, :]
    to_south[STRIP : STRIP + 4, 0:LANES] = west[0:4, :]
    to_south[STRIP : STRIP + 4, LANES:COLS] = east[0:4, :]
    to_north[STRIP + 4 :, :] = jnp.zeros((4, COLS), F32)
    to_south[STRIP + 4 :, :] = jnp.zeros((4, COLS), F32)


def at_all(out, slots, rows, value):
    for slot in range(slots):
        out[slot, rows, :] = value


def side_of(tile, k):
    return turned(tile, 4 * k + 2)


def packed_side(sides):
    lane = lane_iota(8)
    packed = jnp.zeros((8, LANES), F32)
    for k, side in enumerate(sides):
        packed = jnp.where((lane >= 4 * k) & (lane < 4 * k + 4), side_of(side, k), packed)
    return packed


def pack_into(out, index, x):
    out[index, 0:EROWS, :] = x[:, 0:LANES]
    out[index, EROWS : 2 * EROWS, :] = x[:, LANES:COLS]
    sides = [x[8 * k : 8 * k + 8, COLS:ECOLS] for k in range(EROWS // 8)]
    out[index, 2 * EROWS : PACKED, :] = packed_side(sides)


def unpack_into(out, packed):
    out[:, 0:LANES] = packed[0:EROWS]
    out[:, LANES:COLS] = packed[EROWS : 2 * EROWS]
    side = packed[2 * EROWS : PACKED]
    lane = lane_iota(8)
    here = (lane < NARROW) | (lane >= LANES - NARROW)
    for k in range(EROWS // 8):
        out[8 * k : 8 * k + 8, COLS:ECOLS] = jnp.where(here, turned(side, -(4 * k + 2)), 0.0)


def picked(received, keep):
    total = jnp.zeros(received.shape[1:], F32)
    for slot in range(received.shape[0]):
        total = total + jnp.where(keep(slot), received[slot], 0.0)
    return total


def ahead(x, axis):
    return pltpu.roll(x, x.shape[axis] - 1, axis)


def behind(x, axis):
    return pltpu.roll(x, 1, axis)


def rates(flow):
    east, north = flow[0], flow[1]
    return jnp.maximum(-east, 0.0), jnp.maximum(east, 0.0), jnp.maximum(-north, 0.0), jnp.maximum(north, 0.0)


def moves(u):
    return ahead(u, 1), behind(u, 1), ahead(u, 0), behind(u, 0)


def spreading(u):
    e, w, n, s = moves(u)
    return ((e + w) + (n + s)) - 4.0 * u


def drifting(u, rate, out_rate):
    e, w, n, s = moves(u)
    return (rate[0] * e + rate[1] * w + rate[2] * n + rate[3] * s) - out_rate * u


def drifting_back(w, rate, out_rate):
    return (
        behind(rate[0] * w, 1) + ahead(rate[1] * w, 1) + behind(rate[2] * w, 0) + ahead(rate[3] * w, 0)
    ) - out_rate * w


def coeffs(flow, swim, spread):
    rate = rates(flow)
    to = [spread + swim * one for one in rate]
    return 1.0 - (to[0] + to[1] + to[2] + to[3]), *to


def advance(u, coefs, sea):
    centre, to_east, to_west, to_north, to_south = coefs
    e, w, n, s = moves(u)
    return sea * (centre * u + to_east * e + to_west * w + to_north * n + to_south * s)


def retreat(v, coefs):
    centre, to_east, to_west, to_north, to_south = coefs
    return (
        centre * v + behind(to_east * v, 1) + ahead(to_west * v, 1) + behind(to_north * v, 0) + ahead(to_south * v, 0)
    )


def strips(west_in, east_in, north_in, south_in, west, east):
    west[0:ROWS, :] = west_in[...]
    east[0:ROWS, :] = east_in[...]
    west[ROWS : ROWS + 4, :] = north_in[STRIP : STRIP + 4, 0:LANES]
    east[ROWS : ROWS + 4, :] = north_in[STRIP : STRIP + 4, LANES:COLS]
    west[ROWS + 4 : EROWS, :] = south_in[STRIP : STRIP + 4, 0:LANES]
    east[ROWS + 4 : EROWS, :] = south_in[STRIP : STRIP + 4, LANES:COLS]


def own_cells(ref, index, out):
    core = part(ref, index, slice(0, ROWS), slice(0, COLS))
    out[0:ROWS, :] = core[:, 0:LANES]
    out[EROWS : EROWS + ROWS, :] = core[:, LANES:COLS]


def halo_cells(place, west, east, north_in, south_in):
    width = NARROW
    tiles = []
    for half in range(2):
        cols = slice(LANES * half, LANES * half + LANES)
        blank = jnp.zeros((8 - 2 * width, LANES), F32)
        rows = slice(place, place + width)
        tiles.append(jnp.concatenate([north_in[rows, cols], blank, south_in[rows, cols]], axis=0))
    lane = lane_iota(8)
    packed = jnp.zeros((8, LANES), F32)
    for k in range(EROWS // 8):
        rows = slice(8 * k, 8 * k + 8)
        here = (lane >= 4 * k) & (lane < 4 * k + width)
        packed = jnp.where(here, turned(west[rows, :], 4 * k - place), packed)
        here = (lane >= 4 * k + width) & (lane < 4 * k + 4)
        packed = jnp.where(here, turned(east[rows, :], 4 * k + width - place), packed)
    tiles.append(packed)
    return tiles


HALO_ROWS = (ROWS, EROWS + ROWS, 2 * EROWS)


def narrow_field(ref, index, place, west, east, north_in, south_in, out):
    own_cells(ref, index, out)
    for top, tile in zip(HALO_ROWS, halo_cells(place, west, east, north_in, south_in), strict=True):
        out[top : top + 8, :] = tile


def summed_settled(densities, flow, swim, spread, mass):
    sums = [0.0] * 6
    for c in range(N):
        u, d, s = densities[c], spread[c], swim[c]
        factors = (mass[c], mass[c] * d, mass[c] * s, mass[c] * d * d, mass[c] * d * s, mass[c] * s * s)
        sums = [total + factor * u for total, factor in zip(sums, factors, strict=True)]
    rate, sea = rates(flow), flow[2]
    out_rate = (rate[0] + rate[1]) + (rate[2] + rate[3])
    first = [
        sea * (sums[a] + spreading(sums[b]) + drifting(sums[c], rate, out_rate))
        for a, b, c in ((0, 1, 2), (1, 3, 4), (2, 4, 5))
    ]
    return sea * (first[0] + spreading(first[1]) + drifting(first[2], rate, out_rate))


def inner_kernel(density, current_east, current_north, sea_mask, after, swim, spread, mass, total_out):
    del after
    flow = (current_east[...], current_north[...], sea_mask[...].astype(F32))
    total = summed_settled(density, flow, swim, spread, mass)
    slots = total_out.shape[0]
    at_all(total_out, slots, slice(0, ROWS), total[:, 0:LANES])
    at_all(total_out, slots, slice(ROWS, 2 * ROWS), total[:, LANES:COLS])


def ring_of(total):
    row = lax.broadcasted_iota(jnp.int32, (8, LANES), 0)
    outer = (row < 2) | (row >= 6)
    parts = []
    for half in range(2):
        cols = slice(LANES * half, LANES * half + LANES)
        edge = jnp.where(row < 2, total[0:8, cols], total[ROWS - 8 : ROWS, cols])
        parts.append(jnp.where(outer, total[ROWS:EROWS, cols], pltpu.roll(edge, 4, 0)))
    lane = lane_iota(8)
    sides = jnp.zeros((8, LANES), F32)
    for k in range(EROWS // 8):
        rows = slice(8 * k, 8 * k + 8)
        low, high = total[rows, 0:LANES], total[rows, LANES:COLS]
        side = total[rows, COLS:ECOLS]
        base = 8 * k
        for offset, tile, by in (
            (0, high, base - (LANES - 2)),
            (2, side, base + 2),
            (4, side, base + 4 - (LANES - 2)),
            (6, low, base + 6),
        ):
            here = (lane >= base + offset) & (lane < base + offset + 2)
            sides = jnp.where(here, turned(tile, by), sides)
    parts.append(sides)
    return parts


def with_ring(inner, ring, out):
    row = lax.broadcasted_iota(jnp.int32, (8, LANES), 0)
    lane = lane_iota(8)
    sides = ring[16:24]
    for half in range(2):
        lat = ring[8 * half : 8 * half + 8]
        edge = pltpu.roll(lat, 4, 0)
        for k in range(EROWS // 8):
            if k < ROWS // 8:
                tile = inner[ROWS * half + 8 * k : ROWS * half + 8 * k + 8]
            else:
                tile = lat
            if k == 0:
                tile = jnp.where(row < 2, edge, tile)
            if k == ROWS // 8 - 1:
                tile = jnp.where(row >= 6, edge, tile)
            if half == 0:
                tile = jnp.where(lane < 2, turned(sides, -(8 * k + 6)), tile)
            else:
                tile = jnp.where(lane >= LANES - 2, turned(sides, LANES - 2 - 8 * k), tile)
            out[EROWS * half + 8 * k : EROWS * half + 8 * k + 8, :] = tile
    packed = jnp.zeros((8, LANES), F32)
    for k in range(EROWS // 8):
        here = (lane >= 4 * k) & (lane < 4 * k + 2)
        packed = jnp.where(here, turned(sides, -(4 * k + 4)), packed)
        here = (lane >= 4 * k + 2) & (lane < 4 * k + 4)
        packed = jnp.where(here, turned(sides, -4 * k), packed)
    out[2 * EROWS : PACKED, :] = packed


def total_kernel(
    density, current_east, current_north, sea_mask, adjoint, west_in, east_in, north_in, south_in, after, after_too,
    swim, spread, mass, total_out, tail_out, density_out, flow_out, west, east,
):
    del after, after_too
    strips(west_in, east_in, north_in, south_in, west, east)
    narrow_field(adjoint, 0, ADJOINT, west, east, north_in, south_in, tail_out)
    lane = lane_iota(EROWS)
    wide = [(density, c, DENSITY + WIDE * c, density_out.at[c]) for c in range(N)]
    wide += [(current_east, None, EAST, flow_out.at[0]), (current_north, None, NORTH, flow_out.at[1])]
    wide += [(sea_mask, None, SEA, flow_out.at[2])]
    for ref, index, place, out in wide:
        out[0:ROWS, 0:COLS] = part(ref, index, slice(0, ROWS), slice(0, COLS))
        out[ROWS : ROWS + WIDE, 0:COLS] = north_in[place : place + WIDE, :]
        out[EROWS - WIDE : EROWS, 0:COLS] = south_in[place : place + WIDE, :]
        side = jnp.where(lane < WIDE, turned(east[...], -place), 0.0)
        side = jnp.where(lane >= LANES - WIDE, turned(west[...], LANES - WIDE - place), side)
        out[:, COLS:ECOLS] = side
    total = summed_settled(density_out, flow_out, swim, spread, mass)
    for k, ring in enumerate(ring_of(total)):
        at_all(total_out, total_out.shape[0], slice(8 * k, 8 * k + 8), ring)


def fleet_rows(rows, efforts, reported_out, fishing_out, mortality, selectivity):
    harvest = [efforts[f, rows, :] for f in range(N)]
    for f in range(N):
        reported_out[f, rows, :] = reported_out[f, rows, :] * harvest[f]
    for c in range(N):
        fishing = mortality[c] + selectivity[0, c] * harvest[0]
        for f in range(1, N):
            fishing = fishing + selectivity[f, c] * harvest[f]
        fishing_out[c, rows, :] = fishing


def fleet_kernel(
    effort, mask, region, after, mortality, selectivity, fishing_out, reported_out, region_out, efforts
):
    del after
    for k in range(N):
        own_cells(effort, k, efforts.at[k])
        own_cells(mask, k, reported_out.at[k])
    own_cells(region, None, region_out)

    def tile(t, carry):
        for top in (0, EROWS):
            rows = pl.ds(pl.multiple_of(top + t * 8, 8), 8)
            fleet_rows(rows, efforts, reported_out, fishing_out, mortality, selectivity)
        return carry

    lax.fori_loop(0, ROWS // 8, tile, 0)


def settle_kernel(
    fishing, reported, region, adjoint, habitat, west_in, east_in, north_in, south_in, density, flow,
    swim, spread, mortality, selectivity,
    settled_out, fishing_out, reported_out, region_out, carried_out, habitat_out, west, east, efforts,
):
    for source, out in ((fishing, fishing_out), (reported, reported_out), (region, region_out)):
        if SEPARATE:
            out[...] = source[...]
    strips(west_in, east_in, north_in, south_in, west, east)

    def halo(place, out):
        for top, tile in zip(HALO_ROWS, halo_cells(place, west, east, north_in, south_in), strict=True):
            out[top : top + 8, :] = tile

    for k in range(N):
        narrow_field(adjoint, k, ADJOINT + NARROW * k, west, east, north_in, south_in, carried_out.at[k])
        halo(EFFORT + NARROW * k, efforts.at[k])
        halo(MASK + NARROW * k, reported_out.at[k])
    halo(REGION, region_out)
    narrow_field(habitat, None, HABITAT, west, east, north_in, south_in, habitat_out)
    for top in HALO_ROWS:
        fleet_rows(slice(top, top + 8), efforts, reported_out, fishing_out, mortality, selectivity)

    def cohort(c, carry):
        coefs, sea = coeffs(flow, swim[c], spread[c]), flow[2]
        pack_into(settled_out, c, advance(advance(density[c], coefs, sea), coefs, sea))
        return carry

    lax.fori_loop(0, N, cohort, 0)


def catch_kernel(
    age, received, ring, settled, fishing, reported, region, mass, selectivity, mort_out, catch_out, older, fleets
):
    shard = age[0]
    with_ring(picked(received, lambda slot: slot > shard), picked(ring, lambda slot: slot > shard), older)

    def pair(t, carry):
        places = [pl.ds(pl.multiple_of(t * 8, 8), 8), pl.ds(pl.multiple_of(EROWS + t * 8, 8), 8)]
        for rows in places:
            run = older[rows, :]
            taken = [jnp.zeros((8, LANES), F32) for _ in range(N)]
            for c in reversed(range(N)):
                total_mort = fishing[c, rows, :] + 0.02 * run
                mort_out[c, rows, :] = total_mort
                weighted = mass[c] * settled[c, rows, :]
                landed = weighted * ((1.0 - jnp.exp(-total_mort)) / total_mort)
                for f in range(N):
                    taken[f] = taken[f] + selectivity[f, c] * landed
                run = run + weighted
            for f in range(N):
                fleets[f, rows, :] = taken[f] * reported[f, rows, :]
        return carry

    lax.fori_loop(0, EROWS // 8, pair, 0)
    rows = slice(2 * EROWS, PACKED)
    run = older[rows, :]
    for c in reversed(range(N)):
        mort_out[c, rows, :] = fishing[c, rows, :] + 0.02 * run
        run = run + mass[c] * settled[c, rows, :]

    lane = lane_iota(N)
    fleet = lax.broadcasted_iota(jnp.int32, (N, LANES), 0)

    def one_region(r, table):
        sums = [jnp.zeros((8, LANES), F32) for _ in range(N)]
        for half in range(2):
            for t in range(ROWS // 8):
                rows = slice(EROWS * half + 8 * t, EROWS * half + 8 * t + 8)
                here = region[rows, :] == r.astype(F32)
                for f in range(N):
                    sums[f] = sums[f] + jnp.where(here, fleets[f, rows, :], 0.0)
        for f in range(N):
            column = jnp.sum(sums[f], axis=0, keepdims=True)
            column = jnp.sum(column, axis=1, keepdims=True)
            table = jnp.where((fleet == f) & (lane == r + 16 * f), column, table)
        return table

    table = lax.fori_loop(0, 16, one_region, jnp.zeros((N, LANES), F32))
    row = jnp.sum(table, axis=0, keepdims=True)
    catch_out[...] = jnp.broadcast_to(row, catch_out.shape)


def relay_kernel(catches, out):
    out[...] = jnp.broadcast_to(jnp.sum(catches[...], axis=0, keepdims=True), out.shape)


def slope_kernel(
    age, mort, settled, reported, carried, habitat, tail, mass, selectivity,
    still_out, reach_out, kept_out, yield_out, slope_out,
):
    last = age[0] == age[1] - 1

    def tile(t, carry):
        rows = pl.ds(pl.multiple_of(t * 8, 8), 8)
        still = jnp.zeros((8, LANES), F32)
        reach = [jnp.zeros((8, LANES), F32) for _ in range(N)]
        for c in range(N):
            total_mort, settled_c = mort[c, rows, :], settled[c, rows, :]
            survive = jnp.exp(-total_mort)
            yield_frac = (1.0 - survive) / total_mort
            if c + 1 < N:
                coming = carried[c + 1, rows, :]
            else:
                coming = jnp.where(last, carried[c, rows, :], tail[rows, :])
            kept = coming * habitat[rows, :] * survive
            slope = mass[c] * settled_c * (survive - yield_frac) / total_mort
            kept_out[c, rows, :] = kept
            yield_out[c, rows, :] = mass[c] * yield_frac
            slope_out[c, rows, :] = slope
            still = still - kept * settled_c
            for f in range(N):
                reach[f] = reach[f] + selectivity[f, c] * slope
        still_out[rows, :] = still
        for f in range(N):
            reach_out[f, rows, :] = reach[f] * reported[f, rows, :]
        return carry

    lax.fori_loop(0, PACKED // 8, tile, 0)


def press_kernel(catches, observed, region, still, reach, misfit_out, total_out, *, unit):
    predicted = jnp.sum(catches[...], axis=0, keepdims=True) * unit
    misfit = jnp.broadcast_to(1.0 - observed[...] / (1.0 + predicted), (8, LANES))
    misfit_out[...] = misfit
    for t in range(PACKED // 8):
        rows = slice(8 * t, 8 * t + 8)
        place = region[rows, :].astype(jnp.int32)
        total = still[rows, :]
        for f in range(N):
            total = total + jnp.take_along_axis(misfit, place + 16 * f, axis=1) * reach[f, rows, :]
        at_all(total_out, total_out.shape[0], rows, total)


def own_kernel(
    misfit_in, region, reported, settled, kept, yields, slope, flow, swim, spread, mass, selectivity,
    grad_out, bars, wide,
):
    misfit = misfit_in[...]

    def tile(t, carry):
        rows = pl.ds(pl.multiple_of(t * 8, 8), 8)
        place = region[rows, :].astype(jnp.int32)
        spread_back = [
            jnp.take_along_axis(misfit, place + 16 * f, axis=1) * reported[f, rows, :] for f in range(N)
        ]
        run = jnp.zeros((8, LANES), F32)
        for c in range(N):
            pull = selectivity[0, c] * spread_back[0]
            for f in range(1, N):
                pull = pull + selectivity[f, c] * spread_back[f]
            kept_c = kept[c, rows, :]
            bars[c, rows, :] = kept_c + yields[c, rows, :] * pull + (0.02 * mass[c]) * run
            run = run + (slope[c, rows, :] * pull - kept_c * settled[c, rows, :])
        return carry

    lax.fori_loop(0, PACKED // 8, tile, 0)

    def cohort(c, carry):
        coefs, sea = coeffs(flow, swim[c], spread[c]), flow[2]
        unpack_into(wide, bars[c])
        grad_out[c] = retreat(sea * retreat(sea * wide[...], coefs), coefs)[0:ROWS, 0:COLS]
        return carry

    lax.fori_loop(0, N, cohort, 0)


def final_kernel(age, received, own, flow, swim, spread, mass, grad_out, wide, basis):
    shard = age[0]
    unpack_into(wide, picked(received, lambda slot: slot < shard))
    rate, sea = rates(flow), flow[2]
    out_rate = (rate[0] + rate[1]) + (rate[2] + rate[3])
    plain = sea * wide[...]
    spread_once, drift_once = spreading(plain), drifting_back(plain, rate, out_rate)
    spread_sea, drift_sea = sea * spread_once, sea * drift_once
    fields = (
        plain,
        spread_sea + spread_once,
        drift_sea + drift_once,
        spreading(spread_sea),
        spreading(drift_sea) + drifting_back(spread_sea, rate, out_rate),
        drifting_back(drift_sea, rate, out_rate),
    )
    for k, field in enumerate(fields):
        basis[k] = field[0:ROWS, 0:COLS]
    for t in range(ROWS // 8):
        rows = slice(8 * t, 8 * t + 8)
        here = [basis[k, rows, :] for k in range(6)]
        for c in range(N):
            m, d, s = 0.02 * mass[c], spread[c], swim[c]
            younger = m * here[0] + (m * d) * here[1] + (m * s) * here[2]
            younger = younger + (m * d * d) * here[3] + (m * d * s) * here[4] + (m * s * s) * here[5]
            grad_out[c, rows, :] = own[c, rows, :] + younger


VMEM = pl.BlockSpec(memory_space=pltpu.VMEM)
SMEM = pl.BlockSpec(memory_space=pltpu.SMEM)


def shape(*dims):
    return pltpu.VMEM(dims, F32)


def far(*dims):
    return pltpu.HBM(dims, F32)


def near(x):
    return pltpu.with_memory_space_constraint(x, pltpu.VMEM)


def distant(*arrays):
    return [pltpu.with_memory_space_constraint(x, pltpu.HBM) for x in arrays]


def call(kernel, in_specs, outs, scratch=(), aliases=None):
    return pl.pallas_call(
        kernel,
        in_specs=in_specs,
        out_specs=[VMEM] * len(outs),
        out_shape=outs,
        scratch_shapes=[pltpu.VMEM(dims, F32) for dims in scratch],
        input_output_aliases=aliases or {},
        compiler_params=pltpu.CompilerParams(vmem_limit_bytes=24 << 20),
    )


def month(
    density, adjoint_next, current_east, current_north, swim_speed, diffusion, mortality, cohort_mass,
    selectivity, effort, catch_mask, region, sea_mask, habitat, observed,
):
    lons, lats, ages = (lax.axis_size(axis) for axis in ("lon", "lat", "age"))
    age = jnp.stack([lax.axis_index("age"), jnp.int32(ages)])
    inputs = distant(
        density, adjoint_next, effort, catch_mask, current_east, current_north, region, sea_mask, habitat
    )
    density, adjoint_next, effort, catch_mask, current_east, current_north, region, sea_mask, habitat = inputs
    strip_rows = STRIP + 8

    to_east, to_west, to_north, to_south = call(
        pack_kernel,
        [VMEM] * 9,
        [shape(ROWS, LANES), shape(ROWS, LANES), shape(strip_rows, COLS), shape(strip_rows, COLS)],
    )(*inputs)
    from_west = lax.ppermute(to_east, "lon", [(i, (i + 1) % lons) for i in range(lons)])
    from_east = lax.ppermute(to_west, "lon", [((i + 1) % lons, i) for i in range(lons)])
    packed = (PACKED, LANES)
    extended = (EROWS, ECOLS)
    (inner,) = call(
        inner_kernel, [VMEM] * 5 + [SMEM] * 3, [shape(ages, 2 * ROWS, LANES)]
    )(density, current_east, current_north, sea_mask, near(to_east), swim_speed, diffusion, cohort_mass)
    inner = lax.all_to_all(inner, "age", 0, 0, tiled=True)
    to_north, to_south = pl.pallas_call(
        corner_kernel,
        name="corner",
        in_specs=[VMEM] * 4,
        out_specs=[VMEM, VMEM],
        out_shape=[shape(strip_rows, COLS)] * 2,
        input_output_aliases={0: 0, 1: 1},
        compiler_params=pltpu.CompilerParams(vmem_limit_bytes=4 << 20),
    )(near(to_north), near(to_south), near(from_west), near(from_east))
    from_south = lax.ppermute(to_north, "lat", [(i, i + 1) for i in range(lats - 1)])
    from_north = lax.ppermute(to_south, "lat", [(i + 1, i) for i in range(lats - 1)])
    halos = (from_west, from_east, from_north, from_south)

    fishing, reported, regions = call(
        fleet_kernel, [VMEM] * 4 + [SMEM] * 2, [shape(N, *packed)] * 2 + [shape(*packed)], [(N, *packed)]
    )(effort, catch_mask, region, near(to_north), mortality, selectivity)
    ring, tail, density_ext, flow = call(
        total_kernel,
        [VMEM] * 11 + [SMEM] * 3,
        [shape(ages, 24, LANES), shape(*packed), shape(N, *extended), far(3, *extended)],
        [(EROWS, LANES), (EROWS, LANES)],
    )(
        density, current_east, current_north, sea_mask, adjoint_next, *map(near, halos), near(inner), near(regions),
        swim_speed, diffusion, cohort_mass,
    )
    ring = lax.all_to_all(ring, "age", 0, 0, tiled=True)
    tail = lax.ppermute(tail, "age", [(i + 1, i) for i in range(ages - 1)])

    settled, fishing, reported, regions, carried, habitats = call(
        settle_kernel,
        [VMEM] * 11 + [SMEM] * 4,
        [shape(N, *packed)] * 3 + [shape(*packed), far(N, *packed), far(*packed)],
        [(EROWS, LANES), (EROWS, LANES), (N, *packed)],
        {0: 1, 1: 2, 2: 3},
    )(
        near(fishing), near(reported), near(regions), adjoint_next, habitat,
        *distant(*halos), near(density_ext), *distant(flow), swim_speed, diffusion, mortality, selectivity,
    )
    settled, reported, regions = near(settled), near(reported), near(regions)

    mort, catches = call(
        catch_kernel, [SMEM] + [VMEM] * 6 + [SMEM] * 2, [shape(N, *packed), shape(ages, LANES)], [packed, (N, *packed)]
    )(age, near(inner), near(ring), settled, near(fishing), reported, regions, cohort_mass, selectivity)
    catches = near(lax.all_to_all(catches, "age", 0, 0, tiled=True))
    (catches,) = call(relay_kernel, [VMEM], [shape(lons * lats, LANES)])(catches)
    catches = near(lax.all_to_all(catches, ("lon", "lat"), 0, 0, tiled=True))

    still, reach, kept, yields, slope = call(
        slope_kernel, [SMEM] + [VMEM] * 6 + [SMEM] * 2, [shape(*packed), shape(N, *packed)] + [far(N, *packed)] * 3
    )(age, near(mort), settled, reported, *distant(carried, habitats), near(tail), cohort_mass, selectivity)

    unit = observed.shape[1] / (ROWS * COLS * lons * lats)
    misfit, totals = call(
        functools.partial(press_kernel, unit=unit), [VMEM] * 5, [shape(8, LANES), shape(ages, *packed)]
    )(catches, observed.reshape(1, LANES), regions, near(still), near(reach))
    totals = lax.all_to_all(totals, "age", 0, 0, tiled=True)

    kept, yields, slope, flow = distant(kept, yields, slope, flow)
    (own,) = call(
        own_kernel, [VMEM] * 8 + [SMEM] * 4, [shape(N, ROWS, COLS)], [(N, *packed), extended]
    )(near(misfit), regions, reported, settled, kept, yields, slope, flow, swim_speed, diffusion, cohort_mass, selectivity)
    (grad,) = call(
        final_kernel, [SMEM] + [VMEM] * 3 + [SMEM] * 3, [far(N, ROWS, COLS)], [extended, (6, ROWS, COLS)]
    )(age, near(totals), near(own), flow, swim_speed, diffusion, cohort_mass)
    return grad


def solution(mesh):
    placed = (
        P("age", "lat", "lon"),
        P("age", "lat", "lon"),
        P("lat", "lon"),
        P("lat", "lon"),
        P("age"),
        P("age"),
        P("age"),
        P("age"),
        P(None, "age"),
        P(None, "lat", "lon"),
        P(None, "lat", "lon"),
        P("lat", "lon"),
        P("lat", "lon"),
        P("lat", "lon"),
        P(),
    )
    return jax.shard_map(month, mesh=mesh, in_specs=placed, out_specs=P("age", "lat", "lon"), check_vma=False)
```

```python
import functools

import jax
import jax.numpy as jnp
from jax import lax
from jax.experimental import pallas as pl
from jax.experimental.pallas import tpu as pltpu
from jax.sharding import PartitionSpec as P


ROWS, COLS = 64, 256
EROWS, ECOLS = ROWS + 8, COLS + 128
LANES = 128
N = 8
WIDE, NARROW = 4, 2
DENSITY, EAST, NORTH, SEA = 0, 32, 36, 40
ADJOINT, EFFORT, MASK, REGION, HABITAT = 44, 60, 76, 92, 94
FIRST_NARROW = ADJOINT
CORNER = FIRST_NARROW
STRIP = 96
WIDE_ROWS, NARROW_ROWS = CORNER + 4, 56
PACKED = 2 * EROWS + 8
F32 = jnp.float32
SEPARATE = False


def every_field(density, adjoint, effort, mask, east, north, region, sea, habitat):
    for c in range(N):
        yield density, c, DENSITY + WIDE * c, WIDE
    yield east, None, EAST, WIDE
    yield north, None, NORTH, WIDE
    yield sea, None, SEA, WIDE
    for c in range(N):
        yield adjoint, c, ADJOINT + NARROW * c, NARROW
    for f in range(N):
        yield effort, f, EFFORT + NARROW * f, NARROW
    for f in range(N):
        yield mask, f, MASK + NARROW * f, NARROW
    yield region, None, REGION, NARROW
    yield habitat, None, HABITAT, NARROW


def part(ref, index, rows, cols):
    block = ref[rows, cols] if index is None else ref[index, rows, cols]
    return block.astype(F32)


def lane_iota(rows):
    return lax.broadcasted_iota(jnp.int32, (rows, LANES), 1)


def turned(block, by):
    by = by % LANES
    return block if by == 0 else pltpu.roll(block, by, 1)


def pack_kernel(*refs):
    inputs, (to_east, to_west) = refs[:9], refs[9:]
    lane = lane_iota(ROWS)
    everything = slice(0, ROWS)
    right = jnp.zeros((ROWS, LANES), F32)
    left = jnp.zeros((ROWS, LANES), F32)
    for ref, index, place, width in every_field(*inputs):
        here = (lane >= place) & (lane < place + width)
        right = jnp.where(here, turned(part(ref, index, everything, slice(LANES, COLS)), place + width), right)
        left = jnp.where(here, turned(part(ref, index, everything, slice(0, LANES)), place), left)
    to_east[...] = right
    to_west[...] = left


def rows_kernel(*refs):
    inputs, north, south = refs[:9], refs[10:12], refs[12:14]
    for ref, index, place, width in every_field(*inputs):
        narrow = place >= FIRST_NARROW
        at = place - FIRST_NARROW if narrow else place
        north[narrow][at : at + width, :] = part(ref, index, slice(ROWS - width, ROWS), slice(0, COLS))
        south[narrow][at : at + width, :] = part(ref, index, slice(0, width), slice(0, COLS))
    used = STRIP - FIRST_NARROW
    for out in (north[1], south[1]):
        out[used:NARROW_ROWS, :] = jnp.zeros((NARROW_ROWS - used, COLS), F32)


def corner_kernel(north_in, south_in, west, east, to_north, to_south):
    if SEPARATE:
        to_north[0:CORNER, :] = north_in[0:CORNER, :]
        to_south[0:CORNER, :] = south_in[0:CORNER, :]
    to_north[CORNER:WIDE_ROWS, 0:LANES] = west[ROWS - 4 : ROWS, :]
    to_north[CORNER:WIDE_ROWS, LANES:COLS] = east[ROWS - 4 : ROWS, :]
    to_south[CORNER:WIDE_ROWS, 0:LANES] = west[0:4, :]
    to_south[CORNER:WIDE_ROWS, LANES:COLS] = east[0:4, :]


def at_all(out, slots, rows, value):
    for slot in range(slots):
        out[slot, rows, :] = value


def side_of(tile, k):
    return turned(tile, 4 * k + 2)


def packed_side(sides):
    lane = lane_iota(8)
    packed = jnp.zeros((8, LANES), F32)
    for k, side in enumerate(sides):
        packed = jnp.where((lane >= 4 * k) & (lane < 4 * k + 4), side_of(side, k), packed)
    return packed


def pack_into(out, index, x):
    out[index, 0:EROWS, :] = x[:, 0:LANES]
    out[index, EROWS : 2 * EROWS, :] = x[:, LANES:COLS]
    sides = [x[8 * k : 8 * k + 8, COLS:ECOLS] for k in range(EROWS // 8)]
    out[index, 2 * EROWS : PACKED, :] = packed_side(sides)


def unpack_into(out, packed):
    out[:, 0:LANES] = packed[0:EROWS]
    out[:, LANES:COLS] = packed[EROWS : 2 * EROWS]
    side = packed[2 * EROWS : PACKED]
    lane = lane_iota(8)
    here = (lane < NARROW) | (lane >= LANES - NARROW)
    for k in range(EROWS // 8):
        out[8 * k : 8 * k + 8, COLS:ECOLS] = jnp.where(here, turned(side, -(4 * k + 2)), 0.0)


def picked(received, keep):
    total = jnp.zeros(received.shape[1:], F32)
    for slot in range(received.shape[0]):
        total = total + jnp.where(keep(slot), received[slot], 0.0)
    return total


def ahead(x, axis):
    return pltpu.roll(x, x.shape[axis] - 1, axis)


def behind(x, axis):
    return pltpu.roll(x, 1, axis)


def rates(flow):
    east, north = flow[0], flow[1]
    return jnp.maximum(-east, 0.0), jnp.maximum(east, 0.0), jnp.maximum(-north, 0.0), jnp.maximum(north, 0.0)


def moves(u):
    return ahead(u, 1), behind(u, 1), ahead(u, 0), behind(u, 0)


def spreading(u):
    e, w, n, s = moves(u)
    return ((e + w) + (n + s)) - 4.0 * u


def drifting(u, rate, out_rate):
    e, w, n, s = moves(u)
    return (rate[0] * e + rate[1] * w + rate[2] * n + rate[3] * s) - out_rate * u


def drifting_back(w, rate, out_rate):
    return (
        behind(rate[0] * w, 1) + ahead(rate[1] * w, 1) + behind(rate[2] * w, 0) + ahead(rate[3] * w, 0)
    ) - out_rate * w


def coeffs(flow, swim, spread):
    rate = rates(flow)
    to = [spread + swim * one for one in rate]
    return 1.0 - (to[0] + to[1] + to[2] + to[3]), *to


def advance(u, coefs, sea):
    centre, to_east, to_west, to_north, to_south = coefs
    e, w, n, s = moves(u)
    return sea * (centre * u + to_east * e + to_west * w + to_north * n + to_south * s)


def retreat(v, coefs):
    centre, to_east, to_west, to_north, to_south = coefs
    return (
        centre * v + behind(to_east * v, 1) + ahead(to_west * v, 1) + behind(to_north * v, 0) + ahead(to_south * v, 0)
    )


def strips(west_in, east_in, north_in, south_in, west, east):
    west[0:ROWS, :] = west_in[...]
    east[0:ROWS, :] = east_in[...]
    west[ROWS : ROWS + 4, :] = north_in[CORNER:WIDE_ROWS, 0:LANES]
    east[ROWS : ROWS + 4, :] = north_in[CORNER:WIDE_ROWS, LANES:COLS]
    west[ROWS + 4 : EROWS, :] = south_in[CORNER:WIDE_ROWS, 0:LANES]
    east[ROWS + 4 : EROWS, :] = south_in[CORNER:WIDE_ROWS, LANES:COLS]


def own_cells(ref, index, out):
    core = part(ref, index, slice(0, ROWS), slice(0, COLS))
    out[0:ROWS, :] = core[:, 0:LANES]
    out[EROWS : EROWS + ROWS, :] = core[:, LANES:COLS]


def halo_cells(place, west, east, north_in, south_in):
    width = NARROW
    tiles = []
    for half in range(2):
        cols = slice(LANES * half, LANES * half + LANES)
        blank = jnp.zeros((8 - 2 * width, LANES), F32)
        rows = slice(place - FIRST_NARROW, place - FIRST_NARROW + width)
        tiles.append(jnp.concatenate([north_in[rows, cols], blank, south_in[rows, cols]], axis=0))
    lane = lane_iota(8)
    packed = jnp.zeros((8, LANES), F32)
    for k in range(EROWS // 8):
        rows = slice(8 * k, 8 * k + 8)
        here = (lane >= 4 * k) & (lane < 4 * k + width)
        packed = jnp.where(here, turned(west[rows, :], 4 * k - place), packed)
        here = (lane >= 4 * k + width) & (lane < 4 * k + 4)
        packed = jnp.where(here, turned(east[rows, :], 4 * k + width - place), packed)
    tiles.append(packed)
    return tiles


HALO_ROWS = (ROWS, EROWS + ROWS, 2 * EROWS)


def narrow_field(ref, index, place, west, east, north_in, south_in, out):
    own_cells(ref, index, out)
    for top, tile in zip(HALO_ROWS, halo_cells(place, west, east, north_in, south_in), strict=True):
        out[top : top + 8, :] = tile


def summed_settled(densities, flow, swim, spread, mass):
    sums = [0.0] * 6
    for c in range(N):
        u, d, s = densities[c], spread[c], swim[c]
        factors = (mass[c], mass[c] * d, mass[c] * s, mass[c] * d * d, mass[c] * d * s, mass[c] * s * s)
        sums = [total + factor * u for total, factor in zip(sums, factors, strict=True)]
    rate, sea = rates(flow), flow[2]
    out_rate = (rate[0] + rate[1]) + (rate[2] + rate[3])
    first = [
        sea * (sums[a] + spreading(sums[b]) + drifting(sums[c], rate, out_rate))
        for a, b, c in ((0, 1, 2), (1, 3, 4), (2, 4, 5))
    ]
    return sea * (first[0] + spreading(first[1]) + drifting(first[2], rate, out_rate))


def total_kernel(
    density, current_east, current_north, sea_mask, adjoint, west_in, east_in, north_in, south_in,
    narrow_north, narrow_south, after, swim, spread, mass, total_out, tail_out, density_out, flow_out, west, east,
):
    del after
    strips(west_in, east_in, north_in, south_in, west, east)
    narrow_field(adjoint, 0, ADJOINT, west, east, narrow_north, narrow_south, tail_out)
    lane = lane_iota(EROWS)
    wide = [(density, c, DENSITY + WIDE * c, density_out.at[c]) for c in range(N)]
    wide += [(current_east, None, EAST, flow_out.at[0]), (current_north, None, NORTH, flow_out.at[1])]
    wide += [(sea_mask, None, SEA, flow_out.at[2])]
    for ref, index, place, out in wide:
        out[0:ROWS, 0:COLS] = part(ref, index, slice(0, ROWS), slice(0, COLS))
        out[ROWS : ROWS + WIDE, 0:COLS] = north_in[place : place + WIDE, :]
        out[EROWS - WIDE : EROWS, 0:COLS] = south_in[place : place + WIDE, :]
        side = jnp.where(lane < WIDE, turned(east[...], -place), 0.0)
        side = jnp.where(lane >= LANES - WIDE, turned(west[...], LANES - WIDE - place), side)
        out[:, COLS:ECOLS] = side
    total = summed_settled(density_out, flow_out, swim, spread, mass)
    slots = total_out.shape[0]
    at_all(total_out, slots, slice(0, EROWS), total[:, 0:LANES])
    at_all(total_out, slots, slice(EROWS, 2 * EROWS), total[:, LANES:COLS])
    sides = [total[8 * k : 8 * k + 8, COLS:ECOLS] for k in range(EROWS // 8)]
    at_all(total_out, slots, slice(2 * EROWS, PACKED), packed_side(sides))


def fleet_rows(rows, efforts, reported_out, fishing_out, mortality, selectivity):
    harvest = [efforts[f, rows, :] for f in range(N)]
    for f in range(N):
        reported_out[f, rows, :] = reported_out[f, rows, :] * harvest[f]
    for c in range(N):
        fishing = mortality[c] + selectivity[0, c] * harvest[0]
        for f in range(1, N):
            fishing = fishing + selectivity[f, c] * harvest[f]
        fishing_out[c, rows, :] = fishing


def fleet_kernel(
    effort, mask, region, after, mortality, selectivity, fishing_out, reported_out, region_out, efforts
):
    del after
    for k in range(N):
        own_cells(effort, k, efforts.at[k])
        own_cells(mask, k, reported_out.at[k])
    own_cells(region, None, region_out)

    def tile(t, carry):
        for top in (0, EROWS):
            rows = pl.ds(pl.multiple_of(top + t * 8, 8), 8)
            fleet_rows(rows, efforts, reported_out, fishing_out, mortality, selectivity)
        return carry

    lax.fori_loop(0, ROWS // 8, tile, 0)


def settle_kernel(
    fishing, reported, region, adjoint, habitat, west_in, east_in, north_in, south_in,
    narrow_north, narrow_south, density, flow, swim, spread, mortality, selectivity,
    settled_out, fishing_out, reported_out, region_out, carried_out, habitat_out, west, east, efforts,
):
    for source, out in ((fishing, fishing_out), (reported, reported_out), (region, region_out)):
        if SEPARATE:
            out[...] = source[...]
    strips(west_in, east_in, north_in, south_in, west, east)

    def halo(place, out):
        for top, tile in zip(HALO_ROWS, halo_cells(place, west, east, narrow_north, narrow_south), strict=True):
            out[top : top + 8, :] = tile

    for k in range(N):
        narrow_field(adjoint, k, ADJOINT + NARROW * k, west, east, narrow_north, narrow_south, carried_out.at[k])
        halo(EFFORT + NARROW * k, efforts.at[k])
        halo(MASK + NARROW * k, reported_out.at[k])
    halo(REGION, region_out)
    narrow_field(habitat, None, HABITAT, west, east, narrow_north, narrow_south, habitat_out)
    for top in HALO_ROWS:
        fleet_rows(slice(top, top + 8), efforts, reported_out, fishing_out, mortality, selectivity)

    def cohort(c, carry):
        coefs, sea = coeffs(flow, swim[c], spread[c]), flow[2]
        pack_into(settled_out, c, advance(advance(density[c], coefs, sea), coefs, sea))
        return carry

    lax.fori_loop(0, N, cohort, 0)


def catch_kernel(
    age, received, settled, fishing, reported, region, mass, selectivity, mort_out, catch_out, older, fleets
):
    shard = age[0]
    older[...] = picked(received, lambda slot: slot > shard)

    def pair(t, carry):
        places = [pl.ds(pl.multiple_of(t * 8, 8), 8), pl.ds(pl.multiple_of(EROWS + t * 8, 8), 8)]
        for rows in places:
            run = older[rows, :]
            taken = [jnp.zeros((8, LANES), F32) for _ in range(N)]
            for c in reversed(range(N)):
                total_mort = fishing[c, rows, :] + 0.02 * run
                mort_out[c, rows, :] = total_mort
                weighted = mass[c] * settled[c, rows, :]
                landed = weighted * ((1.0 - jnp.exp(-total_mort)) / total_mort)
                for f in range(N):
                    taken[f] = taken[f] + selectivity[f, c] * landed
                run = run + weighted
            for f in range(N):
                fleets[f, rows, :] = taken[f] * reported[f, rows, :]
        return carry

    lax.fori_loop(0, EROWS // 8, pair, 0)
    rows = slice(2 * EROWS, PACKED)
    run = older[rows, :]
    for c in reversed(range(N)):
        mort_out[c, rows, :] = fishing[c, rows, :] + 0.02 * run
        run = run + mass[c] * settled[c, rows, :]

    lane = lane_iota(N)
    fleet = lax.broadcasted_iota(jnp.int32, (N, LANES), 0)

    def one_region(r, table):
        sums = [jnp.zeros((8, LANES), F32) for _ in range(N)]
        for half in range(2):
            for t in range(ROWS // 8):
                rows = slice(EROWS * half + 8 * t, EROWS * half + 8 * t + 8)
                here = region[rows, :] == r.astype(F32)
                for f in range(N):
                    sums[f] = sums[f] + jnp.where(here, fleets[f, rows, :], 0.0)
        for f in range(N):
            column = jnp.sum(sums[f], axis=0, keepdims=True)
            column = jnp.sum(column, axis=1, keepdims=True)
            table = jnp.where((fleet == f) & (lane == r + 16 * f), column, table)
        return table

    table = lax.fori_loop(0, 16, one_region, jnp.zeros((N, LANES), F32))
    row = jnp.sum(table, axis=0, keepdims=True)
    catch_out[...] = jnp.broadcast_to(row, catch_out.shape)


def relay_kernel(catches, out):
    out[...] = jnp.broadcast_to(jnp.sum(catches[...], axis=0, keepdims=True), out.shape)


def slope_kernel(
    age, mort, settled, reported, carried, habitat, tail, mass, selectivity,
    still_out, reach_out, kept_out, yield_out, slope_out,
):
    last = age[0] == age[1] - 1

    def tile(t, carry):
        rows = pl.ds(pl.multiple_of(t * 8, 8), 8)
        still = jnp.zeros((8, LANES), F32)
        reach = [jnp.zeros((8, LANES), F32) for _ in range(N)]
        for c in range(N):
            total_mort, settled_c = mort[c, rows, :], settled[c, rows, :]
            survive = jnp.exp(-total_mort)
            yield_frac = (1.0 - survive) / total_mort
            if c + 1 < N:
                coming = carried[c + 1, rows, :]
            else:
                coming = jnp.where(last, carried[c, rows, :], tail[rows, :])
            kept = coming * habitat[rows, :] * survive
            slope = mass[c] * settled_c * (survive - yield_frac) / total_mort
            kept_out[c, rows, :] = kept
            yield_out[c, rows, :] = mass[c] * yield_frac
            slope_out[c, rows, :] = slope
            still = still - kept * settled_c
            for f in range(N):
                reach[f] = reach[f] + selectivity[f, c] * slope
        still_out[rows, :] = still
        for f in range(N):
            reach_out[f, rows, :] = reach[f] * reported[f, rows, :]
        return carry

    lax.fori_loop(0, PACKED // 8, tile, 0)


def press_kernel(catches, observed, region, still, reach, misfit_out, total_out, *, unit):
    predicted = jnp.sum(catches[...], axis=0, keepdims=True) * unit
    misfit = jnp.broadcast_to(1.0 - observed[...] / (1.0 + predicted), (8, LANES))
    misfit_out[...] = misfit
    for t in range(PACKED // 8):
        rows = slice(8 * t, 8 * t + 8)
        place = region[rows, :].astype(jnp.int32)
        total = still[rows, :]
        for f in range(N):
            total = total + jnp.take_along_axis(misfit, place + 16 * f, axis=1) * reach[f, rows, :]
        at_all(total_out, total_out.shape[0], rows, total)


def own_kernel(
    misfit_in, region, reported, settled, kept, yields, slope, flow, swim, spread, mass, selectivity,
    grad_out, flow_out, bars, wide,
):
    flow_out[...] = flow[...]
    misfit = misfit_in[...]

    def tile(t, carry):
        rows = pl.ds(pl.multiple_of(t * 8, 8), 8)
        place = region[rows, :].astype(jnp.int32)
        spread_back = [
            jnp.take_along_axis(misfit, place + 16 * f, axis=1) * reported[f, rows, :] for f in range(N)
        ]
        run = jnp.zeros((8, LANES), F32)
        for c in range(N):
            pull = selectivity[0, c] * spread_back[0]
            for f in range(1, N):
                pull = pull + selectivity[f, c] * spread_back[f]
            kept_c = kept[c, rows, :]
            bars[c, rows, :] = kept_c + yields[c, rows, :] * pull + (0.02 * mass[c]) * run
            run = run + (slope[c, rows, :] * pull - kept_c * settled[c, rows, :])
        return carry

    lax.fori_loop(0, PACKED // 8, tile, 0)

    def cohort(c, carry):
        coefs, sea = coeffs(flow, swim[c], spread[c]), flow[2]
        unpack_into(wide, bars[c])
        grad_out[c] = retreat(sea * retreat(sea * wide[...], coefs), coefs)[0:ROWS, 0:COLS]
        return carry

    lax.fori_loop(0, N, cohort, 0)


def final_kernel(age, received, own, flow, swim, spread, mass, grad_out, wide, basis):
    shard = age[0]
    unpack_into(wide, picked(received, lambda slot: slot < shard))
    rate, sea = rates(flow), flow[2]
    out_rate = (rate[0] + rate[1]) + (rate[2] + rate[3])
    plain = sea * wide[...]
    spread_once, drift_once = spreading(plain), drifting_back(plain, rate, out_rate)
    spread_sea, drift_sea = sea * spread_once, sea * drift_once
    fields = (
        plain,
        spread_sea + spread_once,
        drift_sea + drift_once,
        spreading(spread_sea),
        spreading(drift_sea) + drifting_back(spread_sea, rate, out_rate),
        drifting_back(drift_sea, rate, out_rate),
    )
    for k, field in enumerate(fields):
        basis[k] = field[0:ROWS, 0:COLS]
    for t in range(ROWS // 8):
        rows = slice(8 * t, 8 * t + 8)
        here = [basis[k, rows, :] for k in range(6)]
        for c in range(N):
            m, d, s = 0.02 * mass[c], spread[c], swim[c]
            younger = m * here[0] + (m * d) * here[1] + (m * s) * here[2]
            younger = younger + (m * d * d) * here[3] + (m * d * s) * here[4] + (m * s * s) * here[5]
            grad_out[c, rows, :] = own[c, rows, :] + younger


VMEM = pl.BlockSpec(memory_space=pltpu.VMEM)
SMEM = pl.BlockSpec(memory_space=pltpu.SMEM)


def shape(*dims):
    return pltpu.VMEM(dims, F32)


def far(*dims):
    return pltpu.HBM(dims, F32)


def near(x):
    return pltpu.with_memory_space_constraint(x, pltpu.VMEM)


def distant(*arrays):
    return [pltpu.with_memory_space_constraint(x, pltpu.HBM) for x in arrays]


def call(kernel, in_specs, outs, scratch=(), aliases=None):
    return pl.pallas_call(
        kernel,
        in_specs=in_specs,
        out_specs=[VMEM] * len(outs),
        out_shape=outs,
        scratch_shapes=[pltpu.VMEM(dims, F32) for dims in scratch],
        input_output_aliases=aliases or {},
        compiler_params=pltpu.CompilerParams(vmem_limit_bytes=24 << 20),
    )


def month(
    density, adjoint_next, current_east, current_north, swim_speed, diffusion, mortality, cohort_mass,
    selectivity, effort, catch_mask, region, sea_mask, habitat, observed,
):
    lons, lats, ages = (lax.axis_size(axis) for axis in ("lon", "lat", "age"))
    age = jnp.stack([lax.axis_index("age"), jnp.int32(ages)])
    inputs = distant(
        density, adjoint_next, effort, catch_mask, current_east, current_north, region, sea_mask, habitat
    )
    density, adjoint_next, effort, catch_mask, current_east, current_north, region, sea_mask, habitat = inputs
    packed = (PACKED, LANES)
    extended = (EROWS, ECOLS)
    to_east, to_west = call(pack_kernel, [VMEM] * 9, [shape(ROWS, LANES)] * 2)(*inputs)
    from_west = lax.ppermute(to_east, "lon", [(i, (i + 1) % lons) for i in range(lons)])
    from_east = lax.ppermute(to_west, "lon", [((i + 1) % lons, i) for i in range(lons)])
    to_north, narrow_north, to_south, narrow_south = call(
        rows_kernel, [VMEM] * 10, [shape(WIDE_ROWS, COLS), shape(NARROW_ROWS, COLS)] * 2
    )(*inputs, near(to_east))
    northward = [(i, i + 1) for i in range(lats - 1)]
    southward = [(i + 1, i) for i in range(lats - 1)]
    narrow_south, narrow_north = (
        lax.ppermute(narrow_north, "lat", northward),
        lax.ppermute(narrow_south, "lat", southward),
    )
    to_north, to_south = call(
        corner_kernel, [VMEM] * 4, [shape(WIDE_ROWS, COLS)] * 2, (), {0: 0, 1: 1}
    )(near(to_north), near(to_south), near(from_west), near(from_east))
    from_south = lax.ppermute(to_north, "lat", northward)
    from_north = lax.ppermute(to_south, "lat", southward)
    halos = (from_west, from_east, from_north, from_south, narrow_north, narrow_south)

    fishing, reported, regions = call(
        fleet_kernel, [VMEM] * 4 + [SMEM] * 2, [shape(N, *packed)] * 2 + [shape(*packed)], [(N, *packed)]
    )(effort, catch_mask, region, near(to_north), mortality, selectivity)
    totals, tail, density_ext, flow = call(
        total_kernel,
        [VMEM] * 12 + [SMEM] * 3,
        [shape(ages, *packed), shape(*packed), shape(N, *extended), far(3, *extended)],
        [(EROWS, LANES), (EROWS, LANES)],
    )(
        density, current_east, current_north, sea_mask, adjoint_next, *map(near, halos), near(regions),
        swim_speed, diffusion, cohort_mass,
    )
    totals = lax.all_to_all(totals, "age", 0, 0, tiled=True)
    tail = lax.ppermute(tail, "age", [(i + 1, i) for i in range(ages - 1)])

    settled, fishing, reported, regions, carried, habitats = call(
        settle_kernel,
        [VMEM] * 13 + [SMEM] * 4,
        [shape(N, *packed)] * 3 + [shape(*packed), far(N, *packed), far(*packed)],
        [(EROWS, LANES), (EROWS, LANES), (N, *packed)],
        {0: 1, 1: 2, 2: 3},
    )(
        near(fishing), near(reported), near(regions), adjoint_next, habitat,
        *distant(*halos), near(density_ext), *distant(flow), swim_speed, diffusion, mortality, selectivity,
    )
    settled, reported, regions = near(settled), near(reported), near(regions)

    mort, catches = call(
        catch_kernel, [SMEM] + [VMEM] * 5 + [SMEM] * 2, [shape(N, *packed), shape(ages, LANES)], [packed, (N, *packed)]
    )(age, near(totals), settled, near(fishing), reported, regions, cohort_mass, selectivity)
    catches = near(lax.all_to_all(catches, "age", 0, 0, tiled=True))
    (catches,) = call(relay_kernel, [VMEM], [shape(lons * lats, LANES)])(catches)
    catches = near(lax.all_to_all(catches, ("lon", "lat"), 0, 0, tiled=True))

    still, reach, kept, yields, slope = call(
        slope_kernel, [SMEM] + [VMEM] * 6 + [SMEM] * 2, [shape(*packed), shape(N, *packed)] + [far(N, *packed)] * 3
    )(age, near(mort), settled, reported, *distant(carried, habitats), near(tail), cohort_mass, selectivity)

    unit = observed.shape[1] / (ROWS * COLS * lons * lats)
    misfit, totals = call(
        functools.partial(press_kernel, unit=unit), [VMEM] * 5, [shape(8, LANES), shape(ages, *packed)]
    )(catches, observed.reshape(1, LANES), regions, near(still), near(reach))
    totals = lax.all_to_all(totals, "age", 0, 0, tiled=True)

    kept, yields, slope, flow = distant(kept, yields, slope, flow)
    own, flow_near = call(
        own_kernel, [VMEM] * 8 + [SMEM] * 4, [shape(N, ROWS, COLS), shape(3, *extended)], [(N, *packed), extended]
    )(near(misfit), regions, reported, settled, kept, yields, slope, flow, swim_speed, diffusion, cohort_mass, selectivity)
    (grad,) = call(
        final_kernel, [SMEM] + [VMEM] * 3 + [SMEM] * 3, [far(N, ROWS, COLS)], [extended, (6, ROWS, COLS)]
    )(age, near(totals), near(own), near(flow_near), swim_speed, diffusion, cohort_mass)
    return grad


def solution(mesh):
    placed = (
        P("age", "lat", "lon"),
        P("age", "lat", "lon"),
        P("lat", "lon"),
        P("lat", "lon"),
        P("age"),
        P("age"),
        P("age"),
        P("age"),
        P(None, "age"),
        P(None, "lat", "lon"),
        P(None, "lat", "lon"),
        P("lat", "lon"),
        P("lat", "lon"),
        P("lat", "lon"),
        P(),
    )
    return jax.shard_map(month, mesh=mesh, in_specs=placed, out_specs=P("age", "lat", "lon"), check_vma=False)
```

```python
import functools

import jax
import jax.numpy as jnp
from jax import lax
from jax.experimental import pallas as pl
from jax.experimental.pallas import tpu as pltpu
from jax.sharding import PartitionSpec as P


ROWS, COLS = 64, 256
EROWS, ECOLS = ROWS + 8, COLS + 128
LANES = 128
N = 8
REGIONS = 16
WIDE, NARROW = 4, 2
DENSITY, EAST, NORTH, SEA = 0, 32, 36, 40
ADJOINT, EFFORT, MASK, REGION, HABITAT = 44, 60, 76, 92, 94
CORNER = 96
STRIP = CORNER + 4
PACKED = 2 * EROWS + 8
F32 = jnp.float32
SEPARATE = False


def every_field(density, adjoint, effort, mask, east, north, region, sea, habitat):
    for c in range(N):
        yield density, c, DENSITY + WIDE * c, WIDE
    yield east, None, EAST, WIDE
    yield north, None, NORTH, WIDE
    yield sea, None, SEA, WIDE
    for c in range(N):
        yield adjoint, c, ADJOINT + NARROW * c, NARROW
    for f in range(N):
        yield effort, f, EFFORT + NARROW * f, NARROW
    for f in range(N):
        yield mask, f, MASK + NARROW * f, NARROW
    yield region, None, REGION, NARROW
    yield habitat, None, HABITAT, NARROW


def part(ref, index, rows, cols):
    block = ref[rows, cols] if index is None else ref[index, rows, cols]
    return block.astype(F32)


def lane_iota(rows):
    return lax.broadcasted_iota(jnp.int32, (rows, LANES), 1)


def turned(block, by):
    by = by % LANES
    return block if by == 0 else pltpu.roll(block, by, 1)


def pack_kernel(*refs):
    inputs, (to_east, to_west, to_north, to_south) = refs[:9], refs[9:]
    lane = lane_iota(ROWS)
    everything = slice(0, ROWS)
    right = jnp.zeros((ROWS, LANES), F32)
    left = jnp.zeros((ROWS, LANES), F32)
    for ref, index, place, width in every_field(*inputs):
        here = (lane >= place) & (lane < place + width)
        right = jnp.where(here, turned(part(ref, index, everything, slice(LANES, COLS)), place + width), right)
        left = jnp.where(here, turned(part(ref, index, everything, slice(0, LANES)), place), left)
        columns = slice(0, COLS)
        to_north[place : place + width, :] = part(ref, index, slice(ROWS - width, ROWS), columns)
        to_south[place : place + width, :] = part(ref, index, slice(0, width), columns)
    to_east[...] = right
    to_west[...] = left


def corner_kernel(north_in, south_in, west, east, to_north, to_south):
    if SEPARATE:
        to_north[0:CORNER, :] = north_in[0:CORNER, :]
        to_south[0:CORNER, :] = south_in[0:CORNER, :]
    to_north[CORNER:STRIP, 0:LANES] = west[ROWS - 4 : ROWS, :]
    to_north[CORNER:STRIP, LANES:COLS] = east[ROWS - 4 : ROWS, :]
    to_south[CORNER:STRIP, 0:LANES] = west[0:4, :]
    to_south[CORNER:STRIP, LANES:COLS] = east[0:4, :]


def at_all(out, slots, rows, value):
    for slot in range(slots):
        out[slot, rows, :] = value


def side_of(tile, k):
    return turned(tile, 4 * k + 2)


def packed_side(sides):
    lane = lane_iota(8)
    packed = jnp.zeros((8, LANES), F32)
    for k, side in enumerate(sides):
        packed = jnp.where((lane >= 4 * k) & (lane < 4 * k + 4), side_of(side, k), packed)
    return packed


def pack_into(out, index, x):
    out[index, 0:EROWS, :] = x[:, 0:LANES]
    out[index, EROWS : 2 * EROWS, :] = x[:, LANES:COLS]
    sides = [x[8 * k : 8 * k + 8, COLS:ECOLS] for k in range(EROWS // 8)]
    out[index, 2 * EROWS : PACKED, :] = packed_side(sides)


def unpack_into(out, packed):
    out[:, 0:LANES] = packed[0:EROWS]
    out[:, LANES:COLS] = packed[EROWS : 2 * EROWS]
    side = packed[2 * EROWS : PACKED]
    lane = lane_iota(8)
    here = (lane < NARROW) | (lane >= LANES - NARROW)
    for k in range(EROWS // 8):
        out[8 * k : 8 * k + 8, COLS:ECOLS] = jnp.where(here, turned(side, -(4 * k + 2)), 0.0)


def picked(received, keep):
    total = jnp.zeros(received.shape[1:], F32)
    for slot in range(received.shape[0]):
        total = total + jnp.where(keep(slot), received[slot], 0.0)
    return total


def ahead(x, axis):
    return pltpu.roll(x, x.shape[axis] - 1, axis)


def behind(x, axis):
    return pltpu.roll(x, 1, axis)


def rates(flow):
    east, north = flow[0], flow[1]
    return jnp.maximum(-east, 0.0), jnp.maximum(east, 0.0), jnp.maximum(-north, 0.0), jnp.maximum(north, 0.0)


def moves(u):
    return ahead(u, 1), behind(u, 1), ahead(u, 0), behind(u, 0)


def spreading(u):
    e, w, n, s = moves(u)
    return ((e + w) + (n + s)) - 4.0 * u


def drifting(u, rate, out_rate):
    e, w, n, s = moves(u)
    return (rate[0] * e + rate[1] * w + rate[2] * n + rate[3] * s) - out_rate * u


def drifting_back(w, rate, out_rate):
    return (
        behind(rate[0] * w, 1) + ahead(rate[1] * w, 1) + behind(rate[2] * w, 0) + ahead(rate[3] * w, 0)
    ) - out_rate * w


def coeffs(flow, swim, spread):
    rate = rates(flow)
    to = [spread + swim * one for one in rate]
    return 1.0 - (to[0] + to[1] + to[2] + to[3]), *to


def advance(u, coefs, sea):
    centre, to_east, to_west, to_north, to_south = coefs
    e, w, n, s = moves(u)
    return sea * (centre * u + to_east * e + to_west * w + to_north * n + to_south * s)


def retreat(v, coefs):
    centre, to_east, to_west, to_north, to_south = coefs
    return (
        centre * v + behind(to_east * v, 1) + ahead(to_west * v, 1) + behind(to_north * v, 0) + ahead(to_south * v, 0)
    )


def strips(west_in, east_in, north_in, south_in, west, east):
    west[0:ROWS, :] = west_in[...]
    east[0:ROWS, :] = east_in[...]
    west[ROWS : ROWS + 4, :] = north_in[CORNER:STRIP, 0:LANES]
    east[ROWS : ROWS + 4, :] = north_in[CORNER:STRIP, LANES:COLS]
    west[ROWS + 4 : EROWS, :] = south_in[CORNER:STRIP, 0:LANES]
    east[ROWS + 4 : EROWS, :] = south_in[CORNER:STRIP, LANES:COLS]


def own_cells(ref, index, out):
    core = part(ref, index, slice(0, ROWS), slice(0, COLS))
    out[0:ROWS, :] = core[:, 0:LANES]
    out[EROWS : EROWS + ROWS, :] = core[:, LANES:COLS]


def halo_cells(place, west, east, north_in, south_in):
    width = NARROW
    tiles = []
    for half in range(2):
        cols = slice(LANES * half, LANES * half + LANES)
        blank = jnp.zeros((8 - 2 * width, LANES), F32)
        rows = slice(place, place + width)
        tiles.append(jnp.concatenate([north_in[rows, cols], blank, south_in[rows, cols]], axis=0))
    lane = lane_iota(8)
    packed = jnp.zeros((8, LANES), F32)
    for k in range(EROWS // 8):
        rows = slice(8 * k, 8 * k + 8)
        here = (lane >= 4 * k) & (lane < 4 * k + width)
        packed = jnp.where(here, turned(west[rows, :], 4 * k - place), packed)
        here = (lane >= 4 * k + width) & (lane < 4 * k + 4)
        packed = jnp.where(here, turned(east[rows, :], 4 * k + width - place), packed)
    tiles.append(packed)
    return tiles


HALO_ROWS = (ROWS, EROWS + ROWS, 2 * EROWS)


def narrow_field(ref, index, place, west, east, north_in, south_in, out):
    own_cells(ref, index, out)
    for top, tile in zip(HALO_ROWS, halo_cells(place, west, east, north_in, south_in), strict=True):
        out[top : top + 8, :] = tile


def summed_settled(densities, flow, swim, spread, mass):
    sums = [0.0] * 6
    for c in range(N):
        u, d, s = densities[c], spread[c], swim[c]
        factors = (mass[c], mass[c] * d, mass[c] * s, mass[c] * d * d, mass[c] * d * s, mass[c] * s * s)
        sums = [total + factor * u for total, factor in zip(sums, factors, strict=True)]
    rate, sea = rates(flow), flow[2]
    out_rate = (rate[0] + rate[1]) + (rate[2] + rate[3])
    first = [
        sea * (sums[a] + spreading(sums[b]) + drifting(sums[c], rate, out_rate))
        for a, b, c in ((0, 1, 2), (1, 3, 4), (2, 4, 5))
    ]
    return sea * (first[0] + spreading(first[1]) + drifting(first[2], rate, out_rate))


def inner_kernel(density, current_east, current_north, sea_mask, after, swim, spread, mass, inner_out):
    del after
    flow = (current_east[...], current_north[...], sea_mask[...].astype(F32))
    inner_out[...] = summed_settled(density, flow, swim, spread, mass)


def wide_fields(density, current_east, current_north, sea_mask):
    for c in range(N):
        yield density, c, DENSITY + WIDE * c
    yield current_east, None, EAST
    yield current_north, None, NORTH
    yield sea_mask, None, SEA


def lat_tile(north_in, south_in, place):
    rows = slice(place, place + WIDE)
    return jnp.concatenate([north_in[rows, :], south_in[rows, :]], axis=0)


def total_kernel(
    density, current_east, current_north, sea_mask, adjoint, west_in, east_in, north_in, south_in, after, inner, swim, spread, mass, total_out, tail_out, west, east,
):
    del after
    strips(west_in, east_in, north_in, south_in, west, east)
    narrow_field(adjoint, 0, ADJOINT, west, east, north_in, south_in, tail_out)
    lane = lane_iota(EROWS)
    half = LANES // 2
    row_band, lane_band = [], []
    for ref, index, place in wide_fields(density, current_east, current_north, sea_mask):
        lat = lat_tile(north_in, south_in, place)
        everything, whole = slice(0, ROWS), slice(0, COLS)
        top = part(ref, index, slice(ROWS - 8, ROWS), whole)
        bottom = part(ref, index, slice(0, 8), whole)
        row_band.append(jnp.concatenate([top, lat, bottom], axis=0))
        low = part(ref, index, everything, slice(0, LANES))
        high = part(ref, index, everything, slice(LANES, COLS))
        low = jnp.concatenate([low, lat[:, 0:LANES]], axis=0)
        high = jnp.concatenate([high, lat[:, LANES:COLS]], axis=0)
        band = jnp.where(lane < half // 2, low, turned(high, half))
        band = jnp.where(lane >= half, turned(east[...], half - place), band)
        band = jnp.where(lane >= half + half // 2, turned(west[...], LANES - WIDE - place), band)
        lane_band.append(band)
    rows_total = summed_settled(row_band[0:N], row_band[N:], swim, spread, mass)
    sides_total = summed_settled(lane_band[0:N], lane_band[N:], swim, spread, mass)
    slots = total_out.shape[0]
    row = lax.broadcasted_iota(jnp.int32, (8, LANES), 0)
    lane = lane_iota(8)
    packed = jnp.zeros((8, LANES), F32)
    for k in range(EROWS // 8):
        sides = sides_total[8 * k : 8 * k + 8]
        for side in range(2):
            cols = slice(LANES * side, LANES * side + LANES)
            tile = inner[8 * k : 8 * k + 8, cols] if k < ROWS // 8 else rows_total[8:16, cols]
            if k == 0:
                tile = jnp.where(row < 2, rows_total[16:24, cols], tile)
            if k == ROWS // 8 - 1:
                tile = jnp.where(row >= 6, rows_total[0:8, cols], tile)
            if side == 0:
                tile = jnp.where(lane < NARROW, sides, tile)
            else:
                tile = jnp.where(lane >= LANES - NARROW, turned(sides, half), tile)
            at_all(total_out, slots, slice(EROWS * side + 8 * k, EROWS * side + 8 * k + 8), tile)
        here = (lane >= 4 * k) & (lane < 4 * k + 2)
        packed = jnp.where(here, turned(sides, 4 * k + 2), packed)
        here = (lane >= 4 * k + 2) & (lane < 4 * k + 4)
        packed = jnp.where(here, turned(sides, 4 * k + 2 - half), packed)
    at_all(total_out, slots, slice(2 * EROWS, PACKED), packed)


def fleet_rows(rows, efforts, reported_out, fishing_out, mortality, selectivity):
    harvest = [efforts[f, rows, :] for f in range(N)]
    for f in range(N):
        reported_out[f, rows, :] = reported_out[f, rows, :] * harvest[f]
    for c in range(N):
        fishing = mortality[c] + selectivity[0, c] * harvest[0]
        for f in range(1, N):
            fishing = fishing + selectivity[f, c] * harvest[f]
        fishing_out[c, rows, :] = fishing


def fleet_kernel(
    effort, mask, region, after, mortality, selectivity, fishing_out, reported_out, region_out, efforts
):
    del after
    for k in range(N):
        own_cells(effort, k, efforts.at[k])
        own_cells(mask, k, reported_out.at[k])
    own_cells(region, None, region_out)

    def tile(t, carry):
        for top in (0, EROWS):
            rows = pl.ds(pl.multiple_of(top + t * 8, 8), 8)
            fleet_rows(rows, efforts, reported_out, fishing_out, mortality, selectivity)
        return carry

    lax.fori_loop(0, ROWS // 8, tile, 0)


def settle_kernel(
    fishing, reported, region, adjoint, habitat, west_in, east_in, north_in, south_in, density, current_east, current_north, sea_mask, swim, spread, mortality, selectivity,
    settled_out, fishing_out, reported_out, region_out, carried_out, habitat_out, flow_out, west, east, efforts,
    density_ext,
):
    for source, out in ((fishing, fishing_out), (reported, reported_out), (region, region_out)):
        if SEPARATE:
            out[...] = source[...]
    strips(west_in, east_in, north_in, south_in, west, east)

    def halo(place, out):
        for top, tile in zip(HALO_ROWS, halo_cells(place, west, east, north_in, south_in), strict=True):
            out[top : top + 8, :] = tile

    for k in range(N):
        narrow_field(adjoint, k, ADJOINT + NARROW * k, west, east, north_in, south_in, carried_out.at[k])
        halo(EFFORT + NARROW * k, efforts.at[k])
        halo(MASK + NARROW * k, reported_out.at[k])
    halo(REGION, region_out)
    narrow_field(habitat, None, HABITAT, west, east, north_in, south_in, habitat_out)
    for top in HALO_ROWS:
        fleet_rows(slice(top, top + 8), efforts, reported_out, fishing_out, mortality, selectivity)

    lane = lane_iota(EROWS)
    outs = [density_ext.at[c] for c in range(N)] + [flow_out.at[k] for k in range(3)]
    for (ref, index, place), out in zip(
        wide_fields(density, current_east, current_north, sea_mask), outs, strict=True
    ):
        out[0:ROWS, 0:COLS] = part(ref, index, slice(0, ROWS), slice(0, COLS))
        out[ROWS:EROWS, 0:COLS] = lat_tile(north_in, south_in, place)
        side = jnp.where(lane < WIDE, turned(east[...], -place), 0.0)
        side = jnp.where(lane >= LANES - WIDE, turned(west[...], LANES - WIDE - place), side)
        out[:, COLS:ECOLS] = side

    def cohort(c, carry):
        coefs, sea = coeffs(flow_out, swim[c], spread[c]), flow_out[2]
        pack_into(settled_out, c, advance(advance(density_ext[c], coefs, sea), coefs, sea))
        return carry

    lax.fori_loop(0, N, cohort, 0)


def catch_kernel(
    age, received, settled, fishing, reported, region, mass, selectivity, mort_out, catch_out, older, fleets, table
):
    shard = age[0]
    older[...] = picked(received, lambda slot: slot > shard)

    def mortality_of(rows):
        run = older[rows, :]
        for c in reversed(range(N)):
            total_mort = fishing[c, rows, :] + 0.02 * run
            mort_out[c, rows, :] = total_mort
            weighted = mass[c] * settled[c, rows, :]
            run = run + weighted
            yield c, total_mort, weighted

    def pair(t, carry):
        for top in (0, EROWS):
            rows = pl.ds(pl.multiple_of(top + t * 8, 8), 8)
            taken = [jnp.zeros((8, LANES), F32) for _ in range(N)]
            for c, total_mort, weighted in mortality_of(rows):
                landed = weighted * ((1.0 - jnp.exp(-total_mort)) / total_mort)
                for f in range(N):
                    taken[f] = taken[f] + selectivity[f, c] * landed
            for f in range(N):
                fleets[f, rows, :] = taken[f] * reported[f, rows, :]
        return carry

    lax.fori_loop(0, ROWS // 8, pair, 0)
    for top in HALO_ROWS:
        for _ in mortality_of(slice(top, top + 8)):
            pass
    half_regions = REGIONS // 2

    def two_regions(r, carry):
        sums = [[jnp.zeros((8, LANES), F32) for _ in range(N)] for _ in range(2)]
        for half in range(2):
            for t in range(ROWS // 8):
                rows = slice(EROWS * half + 8 * t, EROWS * half + 8 * t + 8)
                place = region[rows, :]
                here = [place == (r + k * half_regions).astype(F32) for k in range(2)]
                for f in range(N):
                    fleet = fleets[f, rows, :]
                    for k in range(2):
                        sums[k][f] = sums[k][f] + jnp.where(here[k], fleet, 0.0)
        for f in range(N):
            for k in range(2):
                rows = pl.ds(f * REGIONS + r + k * half_regions, 1)
                table[rows, :] = jnp.sum(sums[k][f], axis=0, keepdims=True)
        return carry

    lax.fori_loop(0, half_regions, two_regions, 0)
    row = jnp.sum(jnp.transpose(table[...]), axis=0, keepdims=True)
    catch_out[...] = jnp.broadcast_to(row, catch_out.shape)


def relay_kernel(catches, out):
    out[...] = jnp.broadcast_to(jnp.sum(catches[...], axis=0, keepdims=True), out.shape)


def slope_kernel(
    age, mort, settled, reported, carried, habitat, tail, mass, selectivity,
    still_out, reach_out, kept_out, yield_out, slope_out,
):
    last = age[0] == age[1] - 1

    def tile(t, carry):
        rows = pl.ds(pl.multiple_of(t * 8, 8), 8)
        still = jnp.zeros((8, LANES), F32)
        reach = [jnp.zeros((8, LANES), F32) for _ in range(N)]
        for c in range(N):
            total_mort, settled_c = mort[c, rows, :], settled[c, rows, :]
            survive = jnp.exp(-total_mort)
            yield_frac = (1.0 - survive) / total_mort
            if c + 1 < N:
                coming = carried[c + 1, rows, :]
            else:
                coming = jnp.where(last, carried[c, rows, :], tail[rows, :])
            kept = coming * habitat[rows, :] * survive
            slope = mass[c] * settled_c * (survive - yield_frac) / total_mort
            kept_out[c, rows, :] = kept
            yield_out[c, rows, :] = mass[c] * yield_frac
            slope_out[c, rows, :] = slope
            still = still - kept * settled_c
            for f in range(N):
                reach[f] = reach[f] + selectivity[f, c] * slope
        still_out[rows, :] = still
        for f in range(N):
            reach_out[f, rows, :] = reach[f] * reported[f, rows, :]
        return carry

    lax.fori_loop(0, PACKED // 8, tile, 0)


def press_kernel(catches, observed, region, still, reach, misfit_out, total_out, *, unit):
    predicted = jnp.sum(catches[...], axis=0, keepdims=True) * unit
    misfit = jnp.broadcast_to(1.0 - observed[...] / (1.0 + predicted), (8, LANES))
    misfit_out[...] = misfit
    for t in range(PACKED // 8):
        rows = slice(8 * t, 8 * t + 8)
        place = region[rows, :].astype(jnp.int32)
        total = still[rows, :]
        for f in range(N):
            total = total + jnp.take_along_axis(misfit, place + 16 * f, axis=1) * reach[f, rows, :]
        at_all(total_out, total_out.shape[0], rows, total)


def own_kernel(
    misfit_in, region, reported, settled, kept, yields, slope, flow, swim, spread, mass, selectivity,
    grad_out, flow_out, bars, wide,
):
    flow_out[...] = flow[...]
    misfit = misfit_in[...]

    def tile(t, carry):
        rows = pl.ds(pl.multiple_of(t * 8, 8), 8)
        place = region[rows, :].astype(jnp.int32)
        spread_back = [
            jnp.take_along_axis(misfit, place + 16 * f, axis=1) * reported[f, rows, :] for f in range(N)
        ]
        run = jnp.zeros((8, LANES), F32)
        for c in range(N):
            pull = selectivity[0, c] * spread_back[0]
            for f in range(1, N):
                pull = pull + selectivity[f, c] * spread_back[f]
            kept_c = kept[c, rows, :]
            bars[c, rows, :] = kept_c + yields[c, rows, :] * pull + (0.02 * mass[c]) * run
            run = run + (slope[c, rows, :] * pull - kept_c * settled[c, rows, :])
        return carry

    lax.fori_loop(0, PACKED // 8, tile, 0)

    def cohort(c, carry):
        coefs, sea = coeffs(flow, swim[c], spread[c]), flow[2]
        unpack_into(wide, bars[c])
        grad_out[c] = retreat(sea * retreat(sea * wide[...], coefs), coefs)[0:ROWS, 0:COLS]
        return carry

    lax.fori_loop(0, N, cohort, 0)


def final_kernel(age, received, own, flow, swim, spread, mass, grad_out, wide, basis):
    shard = age[0]
    unpack_into(wide, picked(received, lambda slot: slot < shard))
    rate, sea = rates(flow), flow[2]
    out_rate = (rate[0] + rate[1]) + (rate[2] + rate[3])
    plain = sea * wide[...]
    spread_once, drift_once = spreading(plain), drifting_back(plain, rate, out_rate)
    spread_sea, drift_sea = sea * spread_once, sea * drift_once
    fields = (
        plain,
        spread_sea + spread_once,
        drift_sea + drift_once,
        spreading(spread_sea),
        spreading(drift_sea) + drifting_back(spread_sea, rate, out_rate),
        drifting_back(drift_sea, rate, out_rate),
    )
    for k, field in enumerate(fields):
        basis[k] = field[0:ROWS, 0:COLS]
    for t in range(ROWS // 8):
        rows = slice(8 * t, 8 * t + 8)
        here = [basis[k, rows, :] for k in range(6)]
        for c in range(N):
            m, d, s = 0.02 * mass[c], spread[c], swim[c]
            younger = m * here[0] + (m * d) * here[1] + (m * s) * here[2]
            younger = younger + (m * d * d) * here[3] + (m * d * s) * here[4] + (m * s * s) * here[5]
            grad_out[c, rows, :] = own[c, rows, :] + younger


VMEM = pl.BlockSpec(memory_space=pltpu.VMEM)
SMEM = pl.BlockSpec(memory_space=pltpu.SMEM)


def shape(*dims):
    return pltpu.VMEM(dims, F32)


def far(*dims):
    return pltpu.HBM(dims, F32)


def near(x):
    return pltpu.with_memory_space_constraint(x, pltpu.VMEM)


def distant(*arrays):
    return [pltpu.with_memory_space_constraint(x, pltpu.HBM) for x in arrays]


def call(kernel, in_specs, outs, scratch=(), aliases=None):
    return pl.pallas_call(
        kernel,
        in_specs=in_specs,
        out_specs=[VMEM] * len(outs),
        out_shape=outs,
        scratch_shapes=[pltpu.VMEM(dims, F32) for dims in scratch],
        input_output_aliases=aliases or {},
        compiler_params=pltpu.CompilerParams(vmem_limit_bytes=24 << 20),
    )


def month(
    density, adjoint_next, current_east, current_north, swim_speed, diffusion, mortality, cohort_mass,
    selectivity, effort, catch_mask, region, sea_mask, habitat, observed,
):
    lons, lats, ages = (lax.axis_size(axis) for axis in ("lon", "lat", "age"))
    age = jnp.stack([lax.axis_index("age"), jnp.int32(ages)])
    inputs = distant(
        density, adjoint_next, effort, catch_mask, current_east, current_north, region, sea_mask, habitat
    )
    density, adjoint_next, effort, catch_mask, current_east, current_north, region, sea_mask, habitat = inputs
    packed = (PACKED, LANES)
    extended = (EROWS, ECOLS)
    to_east, to_west, to_north, to_south = call(
        pack_kernel, [VMEM] * 9, [shape(ROWS, LANES)] * 2 + [shape(STRIP, COLS)] * 2
    )(*inputs)
    from_west = lax.ppermute(to_east, "lon", [(i, (i + 1) % lons) for i in range(lons)])
    from_east = lax.ppermute(to_west, "lon", [((i + 1) % lons, i) for i in range(lons)])
    to_north, to_south = call(
        corner_kernel, [VMEM] * 4, [shape(STRIP, COLS)] * 2, (), {0: 0, 1: 1}
    )(near(to_north), near(to_south), near(from_west), near(from_east))
    from_south = lax.ppermute(to_north, "lat", [(i, i + 1) for i in range(lats - 1)])
    from_north = lax.ppermute(to_south, "lat", [(i + 1, i) for i in range(lats - 1)])
    halos = (from_west, from_east, from_north, from_south)

    fishing, reported, regions = call(
        fleet_kernel, [VMEM] * 4 + [SMEM] * 2, [shape(N, *packed)] * 2 + [shape(*packed)], [(N, *packed)]
    )(effort, catch_mask, region, near(to_north), mortality, selectivity)
    (inner,) = call(inner_kernel, [VMEM] * 5 + [SMEM] * 3, [shape(ROWS, COLS)])(
        density, current_east, current_north, sea_mask, near(to_east), swim_speed, diffusion, cohort_mass
    )
    totals, tail = call(
        total_kernel, [VMEM] * 11 + [SMEM] * 3, [shape(ages, *packed), shape(*packed)], [(EROWS, LANES), (EROWS, LANES)]
    )(
        density, current_east, current_north, sea_mask, adjoint_next, *map(near, halos), near(regions), near(inner),
        swim_speed, diffusion, cohort_mass,
    )
    totals = lax.all_to_all(totals, "age", 0, 0, tiled=True)
    tail = lax.ppermute(tail, "age", [(i + 1, i) for i in range(ages - 1)])

    settled, fishing, reported, regions, carried, habitats, flow = call(
        settle_kernel,
        [VMEM] * 13 + [SMEM] * 4,
        [shape(N, *packed)] * 3 + [shape(*packed), far(N, *packed), far(*packed), far(3, *extended)],
        [(EROWS, LANES), (EROWS, LANES), (N, *packed), (N, *extended)],
        {0: 1, 1: 2, 2: 3},
    )(
        near(fishing), near(reported), near(regions), adjoint_next, habitat,
        *distant(*halos), density, current_east, current_north, sea_mask,
        swim_speed, diffusion, mortality, selectivity,
    )
    settled, reported, regions = near(settled), near(reported), near(regions)

    mort, catches = call(
        catch_kernel,
        [SMEM] + [VMEM] * 5 + [SMEM] * 2,
        [shape(N, *packed), shape(ages, LANES)],
        [packed, (N, *packed), (LANES, LANES)],
    )(age, near(totals), settled, near(fishing), reported, regions, cohort_mass, selectivity)
    catches = near(lax.all_to_all(catches, "age", 0, 0, tiled=True))
    (catches,) = call(relay_kernel, [VMEM], [shape(lons * lats, LANES)])(catches)
    catches = near(lax.all_to_all(catches, ("lon", "lat"), 0, 0, tiled=True))

    still, reach, kept, yields, slope = call(
        slope_kernel, [SMEM] + [VMEM] * 6 + [SMEM] * 2, [shape(*packed), shape(N, *packed)] + [far(N, *packed)] * 3
    )(age, near(mort), settled, reported, *distant(carried, habitats), near(tail), cohort_mass, selectivity)

    unit = observed.shape[1] / (ROWS * COLS * lons * lats)
    misfit, totals = call(
        functools.partial(press_kernel, unit=unit), [VMEM] * 5, [shape(8, LANES), shape(ages, *packed)]
    )(catches, observed.reshape(1, LANES), regions, near(still), near(reach))
    totals = lax.all_to_all(totals, "age", 0, 0, tiled=True)

    kept, yields, slope, flow = distant(kept, yields, slope, flow)
    own, flow_near = call(
        own_kernel, [VMEM] * 8 + [SMEM] * 4, [shape(N, ROWS, COLS), shape(3, *extended)], [(N, *packed), extended]
    )(near(misfit), regions, reported, settled, kept, yields, slope, flow, swim_speed, diffusion, cohort_mass, selectivity)
    (grad,) = call(
        final_kernel, [SMEM] + [VMEM] * 3 + [SMEM] * 3, [far(N, ROWS, COLS)], [extended, (6, ROWS, COLS)]
    )(age, near(totals), near(own), near(flow_near), swim_speed, diffusion, cohort_mass)
    return grad


def solution(mesh):
    placed = (
        P("age", "lat", "lon"),
        P("age", "lat", "lon"),
        P("lat", "lon"),
        P("lat", "lon"),
        P("age"),
        P("age"),
        P("age"),
        P("age"),
        P(None, "age"),
        P(None, "lat", "lon"),
        P(None, "lat", "lon"),
        P("lat", "lon"),
        P("lat", "lon"),
        P("lat", "lon"),
        P(),
    )
    return jax.shard_map(month, mesh=mesh, in_specs=placed, out_specs=P("age", "lat", "lon"), check_vma=False)
```

```python
import functools

import jax
import jax.numpy as jnp
from jax import lax
from jax.experimental import pallas as pl
from jax.experimental.pallas import tpu as pltpu
from jax.sharding import PartitionSpec as P


ROWS, COLS = 64, 256
EROWS, ECOLS = ROWS + 8, COLS + 128
LANES = 128
N = 8
REGIONS = 16
WIDE, NARROW = 4, 2
DENSITY, EAST, NORTH, SEA = 0, 32, 36, 40
ADJOINT, EFFORT, MASK, REGION, HABITAT = 44, 60, 76, 92, 94
CORNER = 96
STRIP = CORNER + 4
LAT, SIDE = 2 * ROWS, 2 * ROWS + 8
PACKED = 2 * ROWS + 16
F32 = jnp.float32
SEPARATE = False


def every_field(density, adjoint, effort, mask, east, north, region, sea, habitat):
    for c in range(N):
        yield density, c, DENSITY + WIDE * c, WIDE
    yield east, None, EAST, WIDE
    yield north, None, NORTH, WIDE
    yield sea, None, SEA, WIDE
    for c in range(N):
        yield adjoint, c, ADJOINT + NARROW * c, NARROW
    for f in range(N):
        yield effort, f, EFFORT + NARROW * f, NARROW
    for f in range(N):
        yield mask, f, MASK + NARROW * f, NARROW
    yield region, None, REGION, NARROW
    yield habitat, None, HABITAT, NARROW


def part(ref, index, rows, cols):
    block = ref[rows, cols] if index is None else ref[index, rows, cols]
    return block.astype(F32)


def lane_iota(rows):
    return lax.broadcasted_iota(jnp.int32, (rows, LANES), 1)


def turned(block, by):
    by = by % LANES
    return block if by == 0 else pltpu.roll(block, by, 1)


FETCH_ORDER = (0, 4, 5, 7, 1, 2, 3, 6, 8)


def pack_kernel(*refs):
    sources, (to_east, to_west, to_north, to_south), inputs, ready = refs[:9], refs[9:13], refs[13:22], refs[22]
    copies = [pltpu.make_async_copy(sources[k], inputs[k], ready.at[k]) for k in range(9)]
    for k in FETCH_ORDER:
        copies[k].start()
    fetched = set()
    lane = lane_iota(ROWS)
    everything = slice(0, ROWS)
    right = jnp.zeros((ROWS, LANES), F32)
    left = jnp.zeros((ROWS, LANES), F32)
    for number, index, place, width in every_field(*range(9)):
        if number not in fetched:
            copies[number].wait()
            fetched.add(number)
        ref = inputs[number]
        here = (lane >= place) & (lane < place + width)
        right = jnp.where(here, turned(part(ref, index, everything, slice(LANES, COLS)), place + width), right)
        left = jnp.where(here, turned(part(ref, index, everything, slice(0, LANES)), place), left)
        columns = slice(0, COLS)
        to_north[place : place + width, :] = part(ref, index, slice(ROWS - width, ROWS), columns)
        to_south[place : place + width, :] = part(ref, index, slice(0, width), columns)
    to_east[...] = right
    to_west[...] = left


def corner_kernel(north_in, south_in, west, east, to_north, to_south):
    if SEPARATE:
        to_north[0:CORNER, :] = north_in[0:CORNER, :]
        to_south[0:CORNER, :] = south_in[0:CORNER, :]
    to_north[CORNER:STRIP, 0:LANES] = west[ROWS - 4 : ROWS, :]
    to_north[CORNER:STRIP, LANES:COLS] = east[ROWS - 4 : ROWS, :]
    to_south[CORNER:STRIP, 0:LANES] = west[0:4, :]
    to_south[CORNER:STRIP, LANES:COLS] = east[0:4, :]


def at_all(out, slots, rows, value):
    for slot in range(slots):
        out[slot, rows, :] = value


def side_of(tile, k):
    return turned(tile, 4 * k + 2)


def packed_side(sides):
    lane = lane_iota(8)
    packed = jnp.zeros((8, LANES), F32)
    for k, side in enumerate(sides):
        packed = jnp.where((lane >= 4 * k) & (lane < 4 * k + 4), side_of(side, k), packed)
    return packed


def merged_lat(first, second):
    row = lax.broadcasted_iota(jnp.int32, (8, LANES), 0)
    return jnp.where((row < NARROW) | (row >= 8 - NARROW), first, pltpu.roll(second, 4, 0))


def pack_into(out, index, x):
    out[index, 0:ROWS, :] = x[0:ROWS, 0:LANES]
    out[index, ROWS : 2 * ROWS, :] = x[0:ROWS, LANES:COLS]
    out[index, LAT : LAT + 8, :] = merged_lat(x[ROWS:EROWS, 0:LANES], x[ROWS:EROWS, LANES:COLS])
    sides = [x[8 * k : 8 * k + 8, COLS:ECOLS] for k in range(EROWS // 8)]
    out[index, SIDE:PACKED, :] = packed_side(sides)


def unpack_into(out, packed):
    out[0:ROWS, 0:LANES] = packed[0:ROWS]
    out[0:ROWS, LANES:COLS] = packed[ROWS : 2 * ROWS]
    lat = packed[LAT : LAT + 8]
    out[ROWS:EROWS, 0:LANES] = lat
    out[ROWS:EROWS, LANES:COLS] = pltpu.roll(lat, 4, 0)
    side = packed[SIDE:PACKED]
    lane = lane_iota(8)
    here = (lane < NARROW) | (lane >= LANES - NARROW)
    for k in range(EROWS // 8):
        out[8 * k : 8 * k + 8, COLS:ECOLS] = jnp.where(here, turned(side, -(4 * k + 2)), 0.0)


def picked(received, keep):
    total = jnp.zeros(received.shape[1:], F32)
    for slot in range(received.shape[0]):
        total = total + jnp.where(keep(slot), received[slot], 0.0)
    return total


def ahead(x, axis):
    return pltpu.roll(x, x.shape[axis] - 1, axis)


def behind(x, axis):
    return pltpu.roll(x, 1, axis)


def rates(flow):
    east, north = flow[0], flow[1]
    return jnp.maximum(-east, 0.0), jnp.maximum(east, 0.0), jnp.maximum(-north, 0.0), jnp.maximum(north, 0.0)


def moves(u):
    return ahead(u, 1), behind(u, 1), ahead(u, 0), behind(u, 0)


def spreading(u):
    e, w, n, s = moves(u)
    return ((e + w) + (n + s)) - 4.0 * u


def drifting(u, rate, out_rate):
    e, w, n, s = moves(u)
    return (rate[0] * e + rate[1] * w + rate[2] * n + rate[3] * s) - out_rate * u


def drifting_back(w, rate, out_rate):
    return (
        behind(rate[0] * w, 1) + ahead(rate[1] * w, 1) + behind(rate[2] * w, 0) + ahead(rate[3] * w, 0)
    ) - out_rate * w


def coeffs(flow, swim, spread):
    rate = rates(flow)
    to = [spread + swim * one for one in rate]
    return 1.0 - (to[0] + to[1] + to[2] + to[3]), *to


def advance(u, coefs, sea):
    centre, to_east, to_west, to_north, to_south = coefs
    e, w, n, s = moves(u)
    return sea * (centre * u + to_east * e + to_west * w + to_north * n + to_south * s)


def retreat(v, coefs):
    centre, to_east, to_west, to_north, to_south = coefs
    return (
        centre * v + behind(to_east * v, 1) + ahead(to_west * v, 1) + behind(to_north * v, 0) + ahead(to_south * v, 0)
    )


def strips(west_in, east_in, north_in, south_in, west, east):
    west[0:ROWS, :] = west_in[...]
    east[0:ROWS, :] = east_in[...]
    west[ROWS : ROWS + 4, :] = north_in[CORNER:STRIP, 0:LANES]
    east[ROWS : ROWS + 4, :] = north_in[CORNER:STRIP, LANES:COLS]
    west[ROWS + 4 : EROWS, :] = south_in[CORNER:STRIP, 0:LANES]
    east[ROWS + 4 : EROWS, :] = south_in[CORNER:STRIP, LANES:COLS]


def own_cells(ref, index, out):
    core = part(ref, index, slice(0, ROWS), slice(0, COLS))
    out[0:ROWS, :] = core[:, 0:LANES]
    out[ROWS : 2 * ROWS, :] = core[:, LANES:COLS]


def halo_cells(place, west, east, north_in, south_in):
    width = NARROW
    rows, low, high = slice(place, place + width), slice(0, LANES), slice(LANES, COLS)
    north_low, south_high, north_high, south_low = (
        north_in[rows, low], south_in[rows, high], north_in[rows, high], south_in[rows, low]
    )
    tiles = [jnp.concatenate([north_low, south_high, north_high, south_low], axis=0)]
    lane = lane_iota(8)
    packed = jnp.zeros((8, LANES), F32)
    for k in range(EROWS // 8):
        rows = slice(8 * k, 8 * k + 8)
        here = (lane >= 4 * k) & (lane < 4 * k + width)
        packed = jnp.where(here, turned(west[rows, :], 4 * k - place), packed)
        here = (lane >= 4 * k + width) & (lane < 4 * k + 4)
        packed = jnp.where(here, turned(east[rows, :], 4 * k + width - place), packed)
    tiles.append(packed)
    return tiles


HALO_ROWS = (LAT, SIDE)


def narrow_field(ref, index, place, west, east, north_in, south_in, out):
    own_cells(ref, index, out)
    for top, tile in zip(HALO_ROWS, halo_cells(place, west, east, north_in, south_in), strict=True):
        out[top : top + 8, :] = tile


def summed_settled(densities, flow, swim, spread, mass):
    sums = [0.0] * 6
    for c in range(N):
        u, d, s = densities[c], spread[c], swim[c]
        factors = (mass[c], mass[c] * d, mass[c] * s, mass[c] * d * d, mass[c] * d * s, mass[c] * s * s)
        sums = [total + factor * u for total, factor in zip(sums, factors, strict=True)]
    rate, sea = rates(flow), flow[2]
    out_rate = (rate[0] + rate[1]) + (rate[2] + rate[3])
    first = [
        sea * (sums[a] + spreading(sums[b]) + drifting(sums[c], rate, out_rate))
        for a, b, c in ((0, 1, 2), (1, 3, 4), (2, 4, 5))
    ]
    return sea * (first[0] + spreading(first[1]) + drifting(first[2], rate, out_rate))


def inner_kernel(
    density, current_east, current_north, sea_mask, adjoint, after, swim, spread, mass,
    inner_out, density_out, east_out, north_out, sea_out, adjoint_out, ready,
):
    del after
    youngest = pltpu.make_async_copy(adjoint.at[0], adjoint_out, ready)
    youngest.start()
    flow = (current_east[...], current_north[...], sea_mask[...].astype(F32))
    inner_out[...] = summed_settled(density, flow, swim, spread, mass)
    density_out[...] = density[...]
    for value, out in zip(flow, (east_out, north_out, sea_out), strict=True):
        out[...] = value
    youngest.wait()


def wide_fields(density, current_east, current_north, sea_mask):
    for c in range(N):
        yield density, c, DENSITY + WIDE * c
    yield current_east, None, EAST
    yield current_north, None, NORTH
    yield sea_mask, None, SEA


def lat_tile(north_in, south_in, place):
    rows = slice(place, place + WIDE)
    return jnp.concatenate([north_in[rows, :], south_in[rows, :]], axis=0)


def total_kernel(
    density, current_east, current_north, sea_mask, adjoint, west_in, east_in, north_in, south_in, after, inner, swim, spread, mass, total_out, tail_out, west, east,
):
    del after
    strips(west_in, east_in, north_in, south_in, west, east)
    narrow_field(adjoint, None, ADJOINT, west, east, north_in, south_in, tail_out)
    lane = lane_iota(EROWS)
    half = LANES // 2
    row_band, lane_band = [], []
    for ref, index, place in wide_fields(density, current_east, current_north, sea_mask):
        lat = lat_tile(north_in, south_in, place)
        everything, whole = slice(0, ROWS), slice(0, COLS)
        top = part(ref, index, slice(ROWS - 8, ROWS), whole)
        bottom = part(ref, index, slice(0, 8), whole)
        row_band.append(jnp.concatenate([top, lat, bottom], axis=0))
        low = part(ref, index, everything, slice(0, LANES))
        high = part(ref, index, everything, slice(LANES, COLS))
        low = jnp.concatenate([low, lat[:, 0:LANES]], axis=0)
        high = jnp.concatenate([high, lat[:, LANES:COLS]], axis=0)
        band = jnp.where(lane < half // 2, low, turned(high, half))
        band = jnp.where(lane >= half, turned(east[...], half - place), band)
        band = jnp.where(lane >= half + half // 2, turned(west[...], LANES - WIDE - place), band)
        lane_band.append(band)
    rows_total = summed_settled(row_band[0:N], row_band[N:], swim, spread, mass)
    sides_total = summed_settled(lane_band[0:N], lane_band[N:], swim, spread, mass)
    slots = total_out.shape[0]
    row = lax.broadcasted_iota(jnp.int32, (8, LANES), 0)
    lane = lane_iota(8)
    lats = []
    packed = jnp.zeros((8, LANES), F32)
    for k in range(EROWS // 8):
        sides = sides_total[8 * k : 8 * k + 8]
        for side in range(2):
            cols = slice(LANES * side, LANES * side + LANES)
            tile = inner[8 * k : 8 * k + 8, cols] if k < ROWS // 8 else rows_total[8:16, cols]
            if k == 0:
                tile = jnp.where(row < 2, rows_total[16:24, cols], tile)
            if k == ROWS // 8 - 1:
                tile = jnp.where(row >= 6, rows_total[0:8, cols], tile)
            if side == 0:
                tile = jnp.where(lane < NARROW, sides, tile)
            else:
                tile = jnp.where(lane >= LANES - NARROW, turned(sides, half), tile)
            if k < ROWS // 8:
                at_all(total_out, slots, slice(ROWS * side + 8 * k, ROWS * side + 8 * k + 8), tile)
            else:
                lats.append(tile)
        here = (lane >= 4 * k) & (lane < 4 * k + 2)
        packed = jnp.where(here, turned(sides, 4 * k + 2), packed)
        here = (lane >= 4 * k + 2) & (lane < 4 * k + 4)
        packed = jnp.where(here, turned(sides, 4 * k + 2 - half), packed)
    at_all(total_out, slots, slice(LAT, LAT + 8), merged_lat(*lats))
    at_all(total_out, slots, slice(SIDE, PACKED), packed)


def fleet_rows(rows, efforts, reported_out, fishing_out, mortality, selectivity):
    harvest = [efforts[f, rows, :] for f in range(N)]
    for f in range(N):
        reported_out[f, rows, :] = reported_out[f, rows, :] * harvest[f]
    for c in range(N):
        fishing = mortality[c] + selectivity[0, c] * harvest[0]
        for f in range(1, N):
            fishing = fishing + selectivity[f, c] * harvest[f]
        fishing_out[c, rows, :] = fishing


def fleet_kernel(
    effort, mask, region, after, mortality, selectivity, fishing_out, reported_out, region_out, efforts
):
    del after
    for k in range(N):
        own_cells(effort, k, efforts.at[k])
        own_cells(mask, k, reported_out.at[k])
    own_cells(region, None, region_out)

    def tile(t, carry):
        for top in (0, ROWS):
            rows = pl.ds(pl.multiple_of(top + t * 8, 8), 8)
            fleet_rows(rows, efforts, reported_out, fishing_out, mortality, selectivity)
        return carry

    lax.fori_loop(0, ROWS // 8, tile, 0)


def settle_kernel(
    fishing, reported, region, adjoint, habitat, west_in, east_in, north_in, south_in, density, current_east, current_north, sea_mask, swim, spread, mortality, selectivity,
    settled_out, fishing_out, reported_out, region_out, carried_out, habitat_out, flow_out, west, east, efforts,
    density_ext,
):
    for source, out in ((fishing, fishing_out), (reported, reported_out), (region, region_out)):
        if SEPARATE:
            out[...] = source[...]
    strips(west_in, east_in, north_in, south_in, west, east)

    def halo(place, out):
        for top, tile in zip(HALO_ROWS, halo_cells(place, west, east, north_in, south_in), strict=True):
            out[top : top + 8, :] = tile

    for k in range(N):
        narrow_field(adjoint, k, ADJOINT + NARROW * k, west, east, north_in, south_in, carried_out.at[k])
        halo(EFFORT + NARROW * k, efforts.at[k])
        halo(MASK + NARROW * k, reported_out.at[k])
    halo(REGION, region_out)
    narrow_field(habitat, None, HABITAT, west, east, north_in, south_in, habitat_out)
    for top in HALO_ROWS:
        fleet_rows(slice(top, top + 8), efforts, reported_out, fishing_out, mortality, selectivity)

    lane = lane_iota(EROWS)
    outs = [density_ext.at[c] for c in range(N)] + [flow_out.at[k] for k in range(3)]
    for (ref, index, place), out in zip(
        wide_fields(density, current_east, current_north, sea_mask), outs, strict=True
    ):
        out[0:ROWS, 0:COLS] = part(ref, index, slice(0, ROWS), slice(0, COLS))
        out[ROWS:EROWS, 0:COLS] = lat_tile(north_in, south_in, place)
        side = jnp.where(lane < WIDE, turned(east[...], -place), 0.0)
        side = jnp.where(lane >= LANES - WIDE, turned(west[...], LANES - WIDE - place), side)
        out[:, COLS:ECOLS] = side

    def cohort(c, carry):
        coefs, sea = coeffs(flow_out, swim[c], spread[c]), flow_out[2]
        pack_into(settled_out, c, advance(advance(density_ext[c], coefs, sea), coefs, sea))
        return carry

    lax.fori_loop(0, N, cohort, 0)


def catch_kernel(
    age, received, settled, fishing, reported, region, mass, selectivity, mort_out, catch_out, older, fleets, table
):
    shard = age[0]
    older[...] = picked(received, lambda slot: slot > shard)

    def mortality_of(rows):
        run = older[rows, :]
        for c in reversed(range(N)):
            total_mort = fishing[c, rows, :] + 0.02 * run
            mort_out[c, rows, :] = total_mort
            weighted = mass[c] * settled[c, rows, :]
            run = run + weighted
            yield c, total_mort, weighted

    def pair(t, carry):
        for top in (0, ROWS):
            rows = pl.ds(pl.multiple_of(top + t * 8, 8), 8)
            taken = [jnp.zeros((8, LANES), F32) for _ in range(N)]
            for c, total_mort, weighted in mortality_of(rows):
                landed = weighted * ((1.0 - jnp.exp(-total_mort)) / total_mort)
                for f in range(N):
                    taken[f] = taken[f] + selectivity[f, c] * landed
            for f in range(N):
                fleets[f, rows, :] = taken[f] * reported[f, rows, :]
        return carry

    lax.fori_loop(0, ROWS // 8, pair, 0)
    for top in HALO_ROWS:
        for _ in mortality_of(slice(top, top + 8)):
            pass
    half_regions = REGIONS // 2

    def two_regions(r, carry):
        sums = [[jnp.zeros((8, LANES), F32) for _ in range(N)] for _ in range(2)]
        for half in range(2):
            for t in range(ROWS // 8):
                rows = slice(ROWS * half + 8 * t, ROWS * half + 8 * t + 8)
                place = region[rows, :]
                here = [place == (r + k * half_regions).astype(F32) for k in range(2)]
                for f in range(N):
                    fleet = fleets[f, rows, :]
                    for k in range(2):
                        sums[k][f] = sums[k][f] + jnp.where(here[k], fleet, 0.0)
        for f in range(N):
            for k in range(2):
                rows = pl.ds(f * REGIONS + r + k * half_regions, 1)
                table[rows, :] = jnp.sum(sums[k][f], axis=0, keepdims=True)
        return carry

    lax.fori_loop(0, half_regions, two_regions, 0)
    row = jnp.sum(jnp.transpose(table[...]), axis=0, keepdims=True)
    catch_out[...] = jnp.broadcast_to(row, catch_out.shape)


def relay_kernel(catches, out):
    out[...] = jnp.broadcast_to(jnp.sum(catches[...], axis=0, keepdims=True), out.shape)


def slope_kernel(
    age, mort, settled, reported, carried, habitat, tail, mass, selectivity,
    still_out, reach_out, kept_out, yield_out, slope_out,
):
    last = age[0] == age[1] - 1

    def tile(t, carry):
        rows = pl.ds(pl.multiple_of(t * 8, 8), 8)
        still = jnp.zeros((8, LANES), F32)
        reach = [jnp.zeros((8, LANES), F32) for _ in range(N)]
        for c in range(N):
            total_mort, settled_c = mort[c, rows, :], settled[c, rows, :]
            survive = jnp.exp(-total_mort)
            yield_frac = (1.0 - survive) / total_mort
            if c + 1 < N:
                coming = carried[c + 1, rows, :]
            else:
                coming = jnp.where(last, carried[c, rows, :], tail[rows, :])
            kept = coming * habitat[rows, :] * survive
            slope = mass[c] * settled_c * (survive - yield_frac) / total_mort
            kept_out[c, rows, :] = kept
            yield_out[c, rows, :] = mass[c] * yield_frac
            slope_out[c, rows, :] = slope
            still = still - kept * settled_c
            for f in range(N):
                reach[f] = reach[f] + selectivity[f, c] * slope
        still_out[rows, :] = still
        for f in range(N):
            reach_out[f, rows, :] = reach[f] * reported[f, rows, :]
        return carry

    lax.fori_loop(0, PACKED // 8, tile, 0)


def press_kernel(catches, observed, region, still, reach, misfit_out, total_out, *, unit):
    predicted = jnp.sum(catches[...], axis=0, keepdims=True) * unit
    misfit = jnp.broadcast_to(1.0 - observed[...] / (1.0 + predicted), (8, LANES))
    misfit_out[...] = misfit
    for t in range(PACKED // 8):
        rows = slice(8 * t, 8 * t + 8)
        place = region[rows, :].astype(jnp.int32)
        total = still[rows, :]
        for f in range(N):
            total = total + jnp.take_along_axis(misfit, place + 16 * f, axis=1) * reach[f, rows, :]
        at_all(total_out, total_out.shape[0], rows, total)


def own_kernel(
    misfit_in, region, reported, settled, kept, yields, slope, flow, swim, spread, mass, selectivity,
    grad_out, flow_out, bars, wide,
):
    flow_out[...] = flow[...]
    misfit = misfit_in[...]

    def tile(t, carry):
        rows = pl.ds(pl.multiple_of(t * 8, 8), 8)
        place = region[rows, :].astype(jnp.int32)
        spread_back = [
            jnp.take_along_axis(misfit, place + 16 * f, axis=1) * reported[f, rows, :] for f in range(N)
        ]
        run = jnp.zeros((8, LANES), F32)
        for c in range(N):
            pull = selectivity[0, c] * spread_back[0]
            for f in range(1, N):
                pull = pull + selectivity[f, c] * spread_back[f]
            kept_c = kept[c, rows, :]
            bars[c, rows, :] = kept_c + yields[c, rows, :] * pull + (0.02 * mass[c]) * run
            run = run + (slope[c, rows, :] * pull - kept_c * settled[c, rows, :])
        return carry

    lax.fori_loop(0, PACKED // 8, tile, 0)

    def cohort(c, carry):
        coefs, sea = coeffs(flow, swim[c], spread[c]), flow[2]
        unpack_into(wide, bars[c])
        grad_out[c] = retreat(sea * retreat(sea * wide[...], coefs), coefs)[0:ROWS, 0:COLS]
        return carry

    lax.fori_loop(0, N, cohort, 0)


def final_kernel(age, received, own, flow, swim, spread, mass, grad_out, wide, basis):
    shard = age[0]
    unpack_into(wide, picked(received, lambda slot: slot < shard))
    rate, sea = rates(flow), flow[2]
    out_rate = (rate[0] + rate[1]) + (rate[2] + rate[3])
    plain = sea * wide[...]
    spread_once, drift_once = spreading(plain), drifting_back(plain, rate, out_rate)
    spread_sea, drift_sea = sea * spread_once, sea * drift_once
    fields = (
        plain,
        spread_sea + spread_once,
        drift_sea + drift_once,
        spreading(spread_sea),
        spreading(drift_sea) + drifting_back(spread_sea, rate, out_rate),
        drifting_back(drift_sea, rate, out_rate),
    )
    for k, field in enumerate(fields):
        basis[k] = field[0:ROWS, 0:COLS]
    for t in range(ROWS // 8):
        rows = slice(8 * t, 8 * t + 8)
        here = [basis[k, rows, :] for k in range(6)]
        for c in range(N):
            m, d, s = 0.02 * mass[c], spread[c], swim[c]
            younger = m * here[0] + (m * d) * here[1] + (m * s) * here[2]
            younger = younger + (m * d * d) * here[3] + (m * d * s) * here[4] + (m * s * s) * here[5]
            grad_out[c, rows, :] = own[c, rows, :] + younger


VMEM = pl.BlockSpec(memory_space=pltpu.VMEM)
SMEM = pl.BlockSpec(memory_space=pltpu.SMEM)


def shape(*dims):
    return pltpu.VMEM(dims, F32)


def far(*dims):
    return pltpu.HBM(dims, F32)


def near(x):
    return pltpu.with_memory_space_constraint(x, pltpu.VMEM)


def distant(*arrays):
    return [pltpu.with_memory_space_constraint(x, pltpu.HBM) for x in arrays]


def call(kernel, in_specs, outs, scratch=(), aliases=None):
    return pl.pallas_call(
        kernel,
        in_specs=in_specs,
        out_specs=[VMEM] * len(outs),
        out_shape=outs,
        scratch_shapes=[pltpu.VMEM(dims, F32) for dims in scratch],
        input_output_aliases=aliases or {},
        compiler_params=pltpu.CompilerParams(vmem_limit_bytes=24 << 20),
    )


def month(
    density, adjoint_next, current_east, current_north, swim_speed, diffusion, mortality, cohort_mass,
    selectivity, effort, catch_mask, region, sea_mask, habitat, observed,
):
    lons, lats, ages = (lax.axis_size(axis) for axis in ("lon", "lat", "age"))
    age = jnp.stack([lax.axis_index("age"), jnp.int32(ages)])
    inputs = distant(
        density, adjoint_next, effort, catch_mask, current_east, current_north, region, sea_mask, habitat
    )
    density, adjoint_next, effort, catch_mask, current_east, current_north, region, sea_mask, habitat = inputs
    packed = (PACKED, LANES)
    extended = (EROWS, ECOLS)
    to_east, to_west, to_north, to_south = pl.pallas_call(
        pack_kernel,
        name="pack",
        in_specs=[pl.BlockSpec(memory_space=pl.ANY)] * 9,
        out_specs=[VMEM] * 4,
        out_shape=[shape(ROWS, LANES)] * 2 + [shape(STRIP, COLS)] * 2,
        scratch_shapes=[pltpu.VMEM(x.shape, x.dtype) for x in inputs] + [pltpu.SemaphoreType.DMA((9,))],
        compiler_params=pltpu.CompilerParams(vmem_limit_bytes=24 << 20),
    )(*inputs)
    from_west = lax.ppermute(to_east, "lon", [(i, (i + 1) % lons) for i in range(lons)])
    from_east = lax.ppermute(to_west, "lon", [((i + 1) % lons, i) for i in range(lons)])
    to_north, to_south = call(
        corner_kernel, [VMEM] * 4, [shape(STRIP, COLS)] * 2, (), {0: 0, 1: 1}
    )(near(to_north), near(to_south), near(from_west), near(from_east))
    from_north = lax.ppermute(to_south, "lat", [(i + 1, i) for i in range(lats - 1)])
    from_south = lax.ppermute(to_north, "lat", [(i, i + 1) for i in range(lats - 1)])
    halos = (from_west, from_east, from_north, from_south)

    fishing, reported, regions = call(
        fleet_kernel, [VMEM] * 4 + [SMEM] * 2, [shape(N, *packed)] * 2 + [shape(*packed)], [(N, *packed)]
    )(effort, catch_mask, region, near(to_north), mortality, selectivity)
    inner, *own_inputs = pl.pallas_call(
        inner_kernel,
        name="inner",
        in_specs=[VMEM] * 4 + [pl.BlockSpec(memory_space=pl.ANY), VMEM] + [SMEM] * 3,
        out_specs=[VMEM] * 6,
        out_shape=[shape(ROWS, COLS), shape(N, ROWS, COLS)] + [shape(ROWS, COLS)] * 4,
        scratch_shapes=[pltpu.SemaphoreType.DMA],
        compiler_params=pltpu.CompilerParams(vmem_limit_bytes=24 << 20),
    )(
        density, current_east, current_north, sea_mask, adjoint_next, near(to_east),
        swim_speed, diffusion, cohort_mass,
    )
    totals, tail = call(
        total_kernel, [VMEM] * 11 + [SMEM] * 3, [shape(ages, *packed), shape(*packed)], [(EROWS, LANES), (EROWS, LANES)]
    )(
        *map(near, own_inputs), *map(near, halos), near(regions), near(inner),
        swim_speed, diffusion, cohort_mass,
    )
    totals = lax.all_to_all(totals, "age", 0, 0, tiled=True)
    tail = lax.ppermute(tail, "age", [(i + 1, i) for i in range(ages - 1)])

    settled, fishing, reported, regions, carried, habitats, flow = call(
        settle_kernel,
        [VMEM] * 13 + [SMEM] * 4,
        [shape(N, *packed)] * 3 + [shape(*packed), far(N, *packed), far(*packed), far(3, *extended)],
        [(EROWS, LANES), (EROWS, LANES), (N, *packed), (N, *extended)],
        {0: 1, 1: 2, 2: 3},
    )(
        near(fishing), near(reported), near(regions), adjoint_next, habitat,
        *distant(*halos), density, current_east, current_north, sea_mask,
        swim_speed, diffusion, mortality, selectivity,
    )
    settled, reported, regions = near(settled), near(reported), near(regions)

    mort, catches = call(
        catch_kernel,
        [SMEM] + [VMEM] * 5 + [SMEM] * 2,
        [shape(N, *packed), shape(ages, LANES)],
        [packed, (N, *packed), (LANES, LANES)],
    )(age, near(totals), settled, near(fishing), reported, regions, cohort_mass, selectivity)
    catches = near(lax.all_to_all(catches, "age", 0, 0, tiled=True))
    (catches,) = call(relay_kernel, [VMEM], [shape(lons * lats, LANES)])(catches)
    catches = near(lax.all_to_all(catches, ("lon", "lat"), 0, 0, tiled=True))

    still, reach, kept, yields, slope = call(
        slope_kernel, [SMEM] + [VMEM] * 6 + [SMEM] * 2, [shape(*packed), shape(N, *packed)] + [far(N, *packed)] * 3
    )(age, near(mort), settled, reported, *distant(carried, habitats), near(tail), cohort_mass, selectivity)

    unit = observed.shape[1] / (ROWS * COLS * lons * lats)
    misfit, totals = call(
        functools.partial(press_kernel, unit=unit), [VMEM] * 5, [shape(8, LANES), shape(ages, *packed)]
    )(catches, observed.reshape(1, LANES), regions, near(still), near(reach))
    totals = lax.all_to_all(totals, "age", 0, 0, tiled=True)

    kept, yields, slope, flow = distant(kept, yields, slope, flow)
    own, flow_near = call(
        own_kernel, [VMEM] * 8 + [SMEM] * 4, [shape(N, ROWS, COLS), shape(3, *extended)], [(N, *packed), extended]
    )(near(misfit), regions, reported, settled, kept, yields, slope, flow, swim_speed, diffusion, cohort_mass, selectivity)
    (grad,) = call(
        final_kernel, [SMEM] + [VMEM] * 3 + [SMEM] * 3, [far(N, ROWS, COLS)], [extended, (6, ROWS, COLS)]
    )(age, near(totals), near(own), near(flow_near), swim_speed, diffusion, cohort_mass)
    return grad


def solution(mesh):
    placed = (
        P("age", "lat", "lon"),
        P("age", "lat", "lon"),
        P("lat", "lon"),
        P("lat", "lon"),
        P("age"),
        P("age"),
        P("age"),
        P("age"),
        P(None, "age"),
        P(None, "lat", "lon"),
        P(None, "lat", "lon"),
        P("lat", "lon"),
        P("lat", "lon"),
        P("lat", "lon"),
        P(),
    )
    return jax.shard_map(month, mesh=mesh, in_specs=placed, out_specs=P("age", "lat", "lon"), check_vma=False)
```
